256 devices in a mesh: seq: 64 (over x, z, core), head: 4 (over y).
Axes of the slice: x: 4, y: 4, z: 8, core: 2. Of those that a mesh axis runs over, the one named last changes fastest.
Arguments:
- query_rows: bfloat16 [32768, 4096], P('seq', 'head'), may hold values from -6 to 6
- key_rows: bfloat16 [32768, 4096], P('seq', 'head'), may hold values from -6 to 6
- value_rows: bfloat16 [32768, 4096], P('seq', 'head'), may hold values from -19 to 19
- norm_gain: float32 [4096], P('head'), may hold values from 0.5 to 1.5
- out_grad: bfloat16 [32768, 4096], P('seq', 'head'), may hold values from -6 to 6
Outputs:
- attn_out: bfloat16 [32768, 4096], P('seq', 'head')
- grad_query: bfloat16 [32768, 4096], P('seq', 'head')
- grad_key: bfloat16 [32768, 4096], P('seq', 'head')
- grad_value: bfloat16 [32768, 4096], P('seq', 'head')
- grad_gain: float32 [4096], P('head')
The draws below stay inside these ranges and needn't reach their ends.
All inputs are finite; a program needn't handle non-finite values.
Results may differ from the reference program's by a relative error of at most 0.0059.
Values sent between devices are 32-bit elements; how exact they have to be, the bound alone decides.
No kernel may reach another device: no remote copies, remote signals or barrier semaphores. Data moves between devices by JAX's collectives and lax.ppermute only.
A program may use at most 128 MiB of HBM per device.

```python
import jax
import jax.numpy as jnp
from jax import lax

HEADS = 32
DH = 128
TOK_DEV = 512
SEQ = 32768
N_SEQ = 64


def draw_value_rows(key, part):
    columns = HEADS * DH
    position = jnp.arange(columns, dtype=jnp.float32) / (columns - 1)
    base = jnp.clip(jax.random.normal(key, (SEQ, columns), jnp.float32), -6.0, 6.0)
    spread = 10.0 ** (0.5 * position)
    return (base * spread[None, :]).astype(jnp.bfloat16)


def level_of(stream_key, dims, cuts, low, largest):
    level, own = 1.0, jax.random.fold_in(stream_key, 6)
    for dim, blocks in cuts:
        draws = jnp.exp(jax.random.uniform(jax.random.fold_in(own, dim), (blocks,), jnp.float32, low / len(cuts), largest / len(cuts)))
        level = level * jnp.repeat(draws, dims[dim] // blocks).reshape([-1 if axis == dim else 1 for axis in range(len(dims))])
    return level


def normal_values(own_key, extent, width, most, cuts=(), kind=jnp.bfloat16):
    drawn = width * jax.random.normal(own_key, extent, jnp.float32)
    if cuts:
        drawn = drawn * level_of(own_key, extent, cuts, -0.22, 0.18)
    return jnp.clip(drawn, -most, most).astype(kind)


def setup_inputs(seed: int = 0) -> dict:
    streams_of = jax.random.split(jax.random.key(seed), 6)
    query_rows = normal_values(streams_of[0], (SEQ, HEADS * DH), 1.0, 6.0, ((0, 64), (1, 4)))
    key_rows = normal_values(streams_of[1], (SEQ, HEADS * DH), 1.0, 6.0, ((0, 64), (1, 4)))
    value_rows = draw_value_rows(jax.random.fold_in(streams_of[5], 71), 0)
    norm_gain = jnp.clip(0.5 + 1.0 * jax.random.uniform(streams_of[3], (HEADS * DH,), jnp.float32) ** level_of(streams_of[3], (HEADS * DH,), ((0, 4),), -0.2, 0.2), 0.5, 1.5)
    out_grad = normal_values(streams_of[4], (SEQ, HEADS * DH), 1.0, 6.0, ((0, 64), (1, 4)))
    return {"query_rows": query_rows, "key_rows": key_rows, "value_rows": value_rows, "norm_gain": norm_gain, "out_grad": out_grad}


norm_eps = 1e-06

def reference(query_rows, key_rows, value_rows, norm_gain, out_grad):
    columns = HEADS * DH
    num_blocks = N_SEQ
    total_rows = num_blocks * TOK_DEV
    query_blocks = query_rows.reshape(num_blocks, TOK_DEV, HEADS, DH)
    key_blocks = key_rows.reshape(num_blocks, TOK_DEV, HEADS, DH)
    value_blocks = value_rows.reshape(num_blocks, TOK_DEV, HEADS, DH)
    causal = jnp.tril(jnp.ones((TOK_DEV, TOK_DEV), dtype=bool))[:, None, :]

    def forward_step(state_sum, pieces):
        query_part, key_part, value_part = pieces
        query_wide = query_part.astype(jnp.float32)
        key_wide = key_part.astype(jnp.float32)
        value_wide = value_part.astype(jnp.float32)
        state_bf = state_sum.astype(jnp.bfloat16)
        scores = jnp.einsum('thd,shd->ths', query_wide, key_wide)
        scores_bf = jnp.where(causal, scores, 0.0).astype(jnp.bfloat16)
        attention = jnp.einsum('thi,hij->thj', query_wide, state_bf.astype(jnp.float32))
        attention = attention + jnp.einsum('ths,shj->thj', scores_bf.astype(jnp.float32), value_wide)
        state_sum = state_sum + jnp.einsum('thi,thj->hij', key_wide, value_wide)
        return (state_sum, (attention, state_bf))
    zero_state = jnp.zeros((HEADS, DH, DH), jnp.float32)
    _, (attention, states_bf) = lax.scan(forward_step, zero_state, (query_blocks, key_blocks, value_blocks))
    attention = attention.reshape(total_rows, columns)
    square_sum = lax.optimization_barrier(jnp.sum(attention * attention, axis=-1))
    inverse = lax.rsqrt(square_sum / columns + norm_eps)
    normed = attention * inverse[:, None]
    attn_out = (normed * norm_gain).astype(jnp.bfloat16)
    grad_wide = out_grad.astype(jnp.float32)
    grad_gain = lax.optimization_barrier(jnp.sum(grad_wide * normed, axis=0))
    scaled = grad_wide * norm_gain
    dot_mean = lax.optimization_barrier(jnp.sum(scaled * attention, axis=-1)) * inverse / columns
    grad_attn = (inverse[:, None] * (scaled - normed * dot_mean[:, None])).astype(jnp.bfloat16)
    grad_blocks = grad_attn.reshape(num_blocks, TOK_DEV, HEADS, DH)

    def backward_step(grad_state, pieces):
        query_part, key_part, value_part, grad_part, state_bf = pieces
        query_wide = query_part.astype(jnp.float32)
        key_wide = key_part.astype(jnp.float32)
        value_wide = value_part.astype(jnp.float32)
        grad_here = grad_part.astype(jnp.float32)
        suffix_bf = grad_state.astype(jnp.bfloat16).astype(jnp.float32)
        scores = jnp.einsum('thd,shd->ths', query_wide, key_wide)
        scores_bf = jnp.where(causal, scores, 0.0).astype(jnp.bfloat16).astype(jnp.float32)
        dscores = jnp.einsum('thj,shj->ths', grad_here, value_wide)
        dscores_bf = jnp.where(causal, dscores, 0.0).astype(jnp.bfloat16).astype(jnp.float32)
        state_wide = state_bf.astype(jnp.float32)
        grad_q = jnp.einsum('thj,hij->thi', grad_here, state_wide) + jnp.einsum('ths,shi->thi', dscores_bf, key_wide)
        grad_k = jnp.einsum('shj,hij->shi', value_wide, suffix_bf) + jnp.einsum('ths,thi->shi', dscores_bf, query_wide)
        grad_v = jnp.einsum('shi,hij->shj', key_wide, suffix_bf) + jnp.einsum('ths,thj->shj', scores_bf, grad_here)
        grad_state = grad_state + jnp.einsum('thi,thj->hij', query_wide, grad_here)
        return (grad_state, (grad_q.astype(jnp.bfloat16), grad_k.astype(jnp.bfloat16), grad_v.astype(jnp.bfloat16)))
    _, (grad_query, grad_key, grad_value) = lax.scan(backward_step, zero_state, (query_blocks, key_blocks, value_blocks, grad_blocks, states_bf), reverse=True)
    grad_query = grad_query.reshape(total_rows, columns)
    grad_key = grad_key.reshape(total_rows, columns)
    grad_value = grad_value.reshape(total_rows, columns)
    return (attn_out, grad_query, grad_key, grad_value, grad_gain)
```

```python
import jax
import jax.numpy as jnp
from jax import lax
from jax.experimental import pallas as pl
from jax.experimental.pallas import tpu as pltpu
from jax.sharding import PartitionSpec as P

HEADS = 32
DH = 128
COLUMNS = HEADS * DH
EPS = 1e-06

f32 = jnp.float32
bf16 = jnp.bfloat16
VMEM = pl.BlockSpec(memory_space=pltpu.VMEM)


def nn(a, b):
    return lax.dot_general(a, b, (((1,), (0,)), ((), ())), preferred_element_type=f32)


def nt(a, b):
    return lax.dot_general(a, b, (((1,), (1,)), ((), ())), preferred_element_type=f32)


def tn(a, b):
    return lax.dot_general(a, b, (((0,), (0,)), ((), ())), preferred_element_type=f32)


def call(kernel, outs, *args):
    return pl.pallas_call(
        kernel,
        out_shape=[jax.ShapeDtypeStruct(s, d) for s, d in outs],
        in_specs=[VMEM] * len(args),
        out_specs=[VMEM] * len(outs),
        compiler_params=pltpu.CompilerParams(vmem_limit_bytes=40 << 20),
    )(*args)


def core_index():
    return lax.rem(lax.axis_index("seq"), 2)


def col(head):
    return pl.ds(pl.multiple_of(head * DH, DH), DH)


def tri(n, upper):
    row = lax.broadcasted_iota(jnp.int32, (n, n), 0)
    column = lax.broadcasted_iota(jnp.int32, (n, n), 1)
    return column >= row if upper else column <= row


def lower_scores(a, b, mask):
    n = a.shape[0] // 2
    top = jnp.where(mask, nt(a[:n], b[:n]), 0.0).astype(bf16)
    left = nt(a[n:], b[:n]).astype(bf16)
    right = jnp.where(mask, nt(a[n:], b[n:]), 0.0).astype(bf16)
    return top, jnp.concatenate([left, right], axis=1)


def upper_scores(a, b, mask):
    n = a.shape[0] // 2
    left = jnp.where(mask, nt(a[:n], b[:n]), 0.0).astype(bf16)
    right = nt(a[:n], b[n:]).astype(bf16)
    bottom = jnp.where(mask, nt(a[n:], b[n:]), 0.0).astype(bf16)
    return jnp.concatenate([left, right], axis=1), bottom


def split_states(core, index, low, high, mine, send):
    rows = pl.ds(pl.multiple_of(index * DH, DH), DH)
    mine[rows, :] = jnp.where(core == 0, low, high)
    send[rows, :] = jnp.where(core == 0, high, low)


def states_kernel(k, v, mine, send):
    half = k.shape[1] // DH // 2
    core = core_index()

    def step(i, _):
        low = tn(k[:, col(i)], v[:, col(i)])
        high = tn(k[:, col(i + half)], v[:, col(i + half)])
        split_states(core, i, low, high, mine, send)
        return 0

    lax.fori_loop(0, half, step, 0)


def local_kernel(q, k, v, out):
    heads = q.shape[1] // DH
    n = q.shape[0] // 2
    mask = tri(n, False)

    def step(h, _):
        top, bottom = lower_scores(q[:, col(h)], k[:, col(h)], mask)
        vh = v[:, col(h)]
        out[:n, col(h)] = nn(top, vh[:n])
        out[n:, col(h)] = nn(bottom, vh)
        return 0

    lax.fori_loop(0, heads, step, 0)


def scan_kernel(reverse, rows, x, out, *total):
    peers = x.shape[0]

    def step(j, run):
        at = peers - 1 - j if reverse else j
        out[at] = run
        return run + x[at, :rows]

    lax.fori_loop(0, peers, step, jnp.zeros(out.shape[1:], f32), unroll=4)
    if total:
        total[0][...] = jnp.sum(x[:, rows:], axis=0)


def attend_kernel(q, local, pre, recv, other, do, gain, att, state_bf, stats):
    half = q.shape[1] // DH // 2
    core = core_index()

    def step(i, sums):
        rows = pl.ds(pl.multiple_of(i * DH, DH), DH)
        own = pre[rows, :] + jnp.where(core == 1, recv[rows, :], 0.0)
        far = other[rows, :]
        low = jnp.where(core == 0, own, far).astype(bf16)
        high = jnp.where(core == 0, far, own).astype(bf16)
        squares, dots = sums
        for h, state in ((i, low), (i + half, high)):
            state_bf[pl.ds(pl.multiple_of(h * DH, DH), DH), :] = state
            a = local[:, col(h)] + nn(q[:, col(h)], state)
            att[:, col(h)] = a
            squares = squares + a * a
            dots = dots + (do[:, col(h)].astype(f32) * gain[:, col(h)]) * a
        return squares, dots

    zero = jnp.zeros((q.shape[0], DH), f32)
    squares, dots = lax.fori_loop(0, half, step, (zero, zero))
    stats[0:1, :] = jnp.sum(squares.T, axis=0, keepdims=True)
    stats[1:2, :] = jnp.sum(dots.T, axis=0, keepdims=True)
    stats[2:8, :] = jnp.zeros((6, q.shape[0]), f32)


def norm_kernel(q, att, do, gain, s0, s1, s2, s3, out, grad, mine, send, gains):
    half = q.shape[1] // DH // 2
    core = core_index()
    tokens = q.shape[0]
    sums = (s0[...] + s1[...] + s2[...] + s3[...]).T
    inverse = lax.rsqrt(sums[:, 0:1] / COLUMNS + EPS)
    mean = sums[:, 1:2] * inverse / COLUMNS
    inverse = jnp.broadcast_to(inverse, (tokens, DH))
    mean = jnp.broadcast_to(mean, (tokens, DH))

    def one(h):
        wide = do[:, col(h)].astype(f32)
        scale = gain[:, col(h)]
        normed = att[:, col(h)] * inverse
        out[:, col(h)] = (normed * scale).astype(bf16)
        gains[:, col(h)] = jnp.sum(wide * normed, axis=0, keepdims=True)
        g = (inverse * (wide * scale - normed * mean)).astype(bf16)
        grad[:, col(h)] = g
        return tn(q[:, col(h)], g)

    def step(i, _):
        low, high = one(i), one(i + half)
        split_states(core, i, low, high, mine, send)
        return 0

    lax.fori_loop(0, half, step, 0)
    send[half * DH :, :] = jnp.concatenate(
        [gains[:, c * DH : (c + 1) * DH] for c in range(2 * half)], axis=0
    )
    mine[half * DH :, :] = send[half * DH :, :]


def query_kernel(grad, k, v, state_bf, out):
    heads = k.shape[1] // DH
    n = k.shape[0] // 2
    mask = tri(n, False)

    def step(h, _):
        g, kh = grad[:, col(h)], k[:, col(h)]
        top, bottom = lower_scores(g, v[:, col(h)], mask)
        far = nt(g, state_bf[pl.ds(pl.multiple_of(h * DH, DH), DH), :])
        out[:n, col(h)] = (far[:n] + nn(top, kh[:n])).astype(bf16)
        out[n:, col(h)] = (far[n:] + nn(bottom, kh)).astype(bf16)
        return 0

    lax.fori_loop(0, heads, step, 0)


def near_kernel(q, k, v, grad, key_near, value_near):
    heads = k.shape[1] // DH
    n = k.shape[0] // 2
    mask = tri(n, True)

    def step(h, _):
        g, qh = grad[:, col(h)], q[:, col(h)]
        top, bottom = upper_scores(v[:, col(h)], g, mask)
        key_near[:n, col(h)] = nn(top, qh)
        key_near[n:, col(h)] = nn(bottom, qh[n:])
        top, bottom = upper_scores(k[:, col(h)], qh, mask)
        value_near[:n, col(h)] = nn(top, g)
        value_near[n:, col(h)] = nn(bottom, g[n:])
        return 0

    lax.fori_loop(0, heads, step, 0)


def finish_kernel(k, v, key_near, value_near, suf, recv, other, grad_key, grad_value):
    half = k.shape[1] // DH // 2
    core = core_index()

    def step(i, _):
        rows = pl.ds(pl.multiple_of(i * DH, DH), DH)
        own = suf[rows, :] + jnp.where(core == 0, recv[rows, :], 0.0)
        far = other[rows, :]
        low = jnp.where(core == 0, own, far).astype(bf16)
        high = jnp.where(core == 0, far, own).astype(bf16)
        for h, state in ((i, low), (i + half, high)):
            key = nt(v[:, col(h)], state) + key_near[:, col(h)]
            grad_key[:, col(h)] = key.astype(bf16)
            value = nn(k[:, col(h)], state) + value_near[:, col(h)]
            grad_value[:, col(h)] = value.astype(bf16)
        return 0

    lax.fori_loop(0, half, step, 0)


def pack_kernel(mine, recv, out):
    peers, rows, _ = out.shape
    states = mine.shape[0] - 8
    near = mine[:states, :] + recv[:states, :]
    out[:, : rows - 8, :] = near.reshape(peers, rows - 8, DH)
    gains = mine[states:, :] + recv[states:, :]
    out[:, rows - 8 :, :] = jnp.broadcast_to(gains[None], (peers, 8, DH))


def body(query_rows, key_rows, value_rows, norm_gain, out_grad):
    q, k, v, do = query_rows, key_rows, value_rows, out_grad
    tokens, width = q.shape
    gain = norm_gain.reshape(1, width)
    peers = lax.axis_size("seq")
    chips = peers // 2
    ring = lax.axis_size("head")
    half = width // DH // 2
    state_rows = half * DH
    slice_rows = state_rows // chips
    swap_pairs = [(i, i ^ 1) for i in range(peers)]
    groups = [[2 * i + c for i in range(chips)] for c in range(2)]
    core = core_index()

    def swap(x):
        return lax.ppermute(x, "seq", swap_pairs)

    def exchange(x):
        return lax.all_to_all(x, "seq", 0, 0, axis_index_groups=groups)

    def scan(x, reverse):
        rows = x.shape[1] - slice_rows
        outs = [((chips, slice_rows, DH), f32)] + ([((rows, DH), f32)] if rows else [])
        kernel = lambda *refs: scan_kernel(reverse, slice_rows, *refs)
        return call(kernel, outs, x)

    state_shape = ((state_rows, DH), f32)
    mine, send = call(states_kernel, [state_shape, state_shape], k, v)
    recv = swap(send)
    (local,) = call(local_kernel, [((tokens, width), f32)], q, k, v)
    (before,) = scan(exchange((mine + recv).reshape(chips, slice_rows, DH)), False)
    before = exchange(before).reshape(state_rows, DH)
    other = swap(jnp.where(core == 0, before + mine, before))
    att, state_bf, stats = call(
        attend_kernel,
        [((tokens, width), f32), ((width, DH), bf16), ((8, tokens), f32)],
        q, local, before, recv, other, do, gain,
    )
    parts = [
        lax.ppermute(stats, "head", [(i, (i + d) % ring) for i in range(ring)])
        for d in range(1, ring)
    ]
    wide_shape = ((state_rows + 8, DH), f32)
    attn_out, grad, mine, send, _ = call(
        norm_kernel,
        [((tokens, width), bf16), ((tokens, width), bf16), wide_shape, wide_shape, ((1, width), f32)],
        q, att, do, gain, stats, *parts,
    )
    recv = swap(send)
    (grad_query,) = call(query_kernel, [((tokens, width), bf16)], grad, k, v, state_bf)
    (packed,) = call(pack_kernel, [((chips, slice_rows + 8, DH), f32)], mine, recv)
    after, grad_gain = scan(exchange(packed), True)
    after = exchange(after).reshape(state_rows, DH)
    other = swap(jnp.where(core == 1, after + mine[:state_rows], after))
    key_near, value_near = call(
        near_kernel, [((tokens, width), f32), ((tokens, width), f32)], q, k, v, grad
    )
    grad_key, grad_value = call(
        finish_kernel,
        [((tokens, width), bf16), ((tokens, width), bf16)],
        k, v, key_near, value_near, after, recv, other,
    )
    return attn_out, grad_query, grad_key, grad_value, grad_gain.reshape(width)


def solution(mesh):
    rows, heads = P("seq", "head"), P("head")
    return jax.shard_map(
        body,
        mesh=mesh,
        in_specs=(rows, rows, rows, heads, rows),
        out_specs=(rows, rows, rows, rows, heads),
        check_vma=False,
    )
```

```python
import functools

import jax
import jax.numpy as jnp
from jax import lax
from jax.experimental import pallas as pl
from jax.experimental.pallas import tpu as pltpu
from jax.sharding import PartitionSpec as P

HEADS = 32
DH = 128
COLUMNS = HEADS * DH
EPS = 1e-06

f32 = jnp.float32
bf16 = jnp.bfloat16
VMEM = pl.BlockSpec(memory_space=pltpu.VMEM)
HBM = pl.BlockSpec(memory_space=pltpu.HBM)


def nn(a, b):
    return lax.dot_general(a, b, (((1,), (0,)), ((), ())), preferred_element_type=f32)


def nt(a, b):
    return lax.dot_general(a, b, (((1,), (1,)), ((), ())), preferred_element_type=f32)


def tn(a, b):
    return lax.dot_general(a, b, (((0,), (0,)), ((), ())), preferred_element_type=f32)


def call(kernel, outs, *args, ins=None, places=None, scratch=(), aliases={}):
    ins = ins or [VMEM] * len(args)
    places = places or [VMEM] * len(outs)
    shapes = [
        pltpu.HBM(s, d) if place is HBM else jax.ShapeDtypeStruct(s, d)
        for (s, d), place in zip(outs, places)
    ]
    args = [
        pltpu.with_memory_space_constraint(x, pltpu.HBM) if place is HBM else x
        for x, place in zip(args, ins)
    ]
    return pl.pallas_call(
        kernel,
        out_shape=shapes,
        in_specs=ins,
        out_specs=places,
        scratch_shapes=scratch,
        input_output_aliases=aliases,
        compiler_params=pltpu.CompilerParams(vmem_limit_bytes=24 << 20),
    )(*args)


def core_index():
    return lax.rem(lax.axis_index("seq"), 2)


def col(head):
    return pl.ds(pl.multiple_of(head * DH, DH), DH)


def tri(n, upper):
    row = lax.broadcasted_iota(jnp.int32, (n, n), 0)
    column = lax.broadcasted_iota(jnp.int32, (n, n), 1)
    return column >= row if upper else column <= row


def lower_scores(a, b, mask):
    n = a.shape[0] // 2
    top = jnp.where(mask, nt(a[:n], b[:n]), 0.0).astype(bf16)
    left = nt(a[n:], b[:n]).astype(bf16)
    right = jnp.where(mask, nt(a[n:], b[n:]), 0.0).astype(bf16)
    return top, jnp.concatenate([left, right], axis=1)


def upper_scores(a, b, mask):
    n = a.shape[0] // 2
    left = jnp.where(mask, nt(a[:n], b[:n]), 0.0).astype(bf16)
    right = nt(a[:n], b[n:]).astype(bf16)
    bottom = jnp.where(mask, nt(a[n:], b[n:]), 0.0).astype(bf16)
    return jnp.concatenate([left, right], axis=1), bottom


def head_rows(head):
    return pl.ds(pl.multiple_of(head * DH, DH), DH)


def fetch(refs, buffers, sems, heads):
    copies = []
    for slot, head in enumerate(heads):
        copies.append([
            pltpu.make_async_copy(ref.at[:, col(head)], buffer.at[slot], sems.at[n, slot])
            for n, (ref, buffer) in enumerate(zip(refs, buffers))
        ])
        for copy in copies[-1]:
            copy.start()
    return copies


def states_kernel(k, v, out, k_buffer, v_buffer, sems):
    heads = k.shape[1] // DH
    copies = fetch((k, v), (k_buffer, v_buffer), sems, range(heads))
    for h in range(heads):
        for copy in copies[h]:
            copy.wait()
        out[h * DH : (h + 1) * DH, :] = tn(k_buffer[h], v_buffer[h])


def add_kernel(states, recv, out):
    rows = out.shape[0] * out.shape[1]
    half = pl.ds(pl.multiple_of(core_index() * rows, rows), rows)
    out[...] = (states[half, :] + recv[half, :]).reshape(out.shape)


def local_kernel(q, k, v, out):
    heads = q.shape[1] // DH
    n = q.shape[0] // 2
    mask = tri(n, False)

    def step(h, _):
        top, bottom = lower_scores(q[:, col(h)], k[:, col(h)], mask)
        vh = v[:, col(h)]
        out[:n, col(h)] = nn(top, vh[:n])
        out[n:, col(h)] = nn(bottom, vh)
        return 0

    lax.fori_loop(0, heads, step, 0, unroll=2)


def scan_kernel(reverse, rows, x, out, *total):
    peers = x.shape[0]

    run = jnp.zeros(out.shape[1:], f32)
    for at in range(peers - 1, -1, -1) if reverse else range(peers):
        out[at] = run
        run = run + x[at, :rows]
    if total:
        total[0][...] = jnp.sum(x[:, rows:], axis=0)


def attend_kernel(q, local, pre, other, recv, do, gain, att, state_bf, stats):
    half = q.shape[1] // DH // 2
    core = core_index()
    later = (core == 1).astype(f32)

    def step(i, sums):
        own, far = pre[head_rows(i), :], other[head_rows(i), :]
        low = jnp.where(core == 0, own, far)
        high = jnp.where(core == 0, far, own)
        squares, dots = sums
        for h, state in ((i, low), (i + half, high)):
            state = (state + later * recv[head_rows(h), :]).astype(bf16)
            state_bf[head_rows(h), :] = state
            a = local[:, col(h)] + nn(q[:, col(h)], state)
            att[:, col(h)] = a
            squares = squares + a * a
            dots = dots + (do[:, col(h)].astype(f32) * gain[:, col(h)]) * a
        return squares, dots

    zero = jnp.zeros((q.shape[0], DH), f32)
    squares, dots = lax.fori_loop(0, half, step, (zero, zero))
    stats[0:1, :] = jnp.sum(squares.T, axis=0, keepdims=True)
    stats[1:2, :] = jnp.sum(dots.T, axis=0, keepdims=True)
    stats[2:8, :] = jnp.zeros((6, q.shape[0]), f32)


def position_factors(s0, s1, s2, s3):
    sums = (s0[...] + s1[...] + s2[...] + s3[...]).T
    inverse = lax.rsqrt(sums[:, 0:1] / COLUMNS + EPS)
    mean = sums[:, 1:2] * inverse / COLUMNS
    shape = (sums.shape[0], DH)
    return jnp.broadcast_to(inverse, shape), jnp.broadcast_to(mean, shape)


def norm_kernel(q, att, do, gain, s0, s1, s2, s3, grad, states, gains):
    heads = q.shape[1] // DH
    inverse, mean = position_factors(s0, s1, s2, s3)

    def step(h, _):
        wide = do[:, col(h)].astype(f32)
        normed = att[:, col(h)] * inverse
        gains[:, col(h)] = jnp.sum(wide * normed, axis=0, keepdims=True)
        g = (inverse * (wide * gain[:, col(h)] - normed * mean)).astype(bf16)
        grad[:, col(h)] = g
        states[head_rows(h), :] = tn(q[:, col(h)], g)
        return 0

    lax.fori_loop(0, heads, step, 0, unroll=2)
    for h in range(heads):
        states[heads * DH + h : heads * DH + h + 1, :] = gains[:, h * DH : (h + 1) * DH]


def output_kernel(att, gain, s0, s1, s2, s3, grad, state_bf, out, grad_out, state_out, rows, sems):
    heads = att.shape[1] // DH
    kept = [
        pltpu.make_async_copy(grad, grad_out, sems.at[heads]),
        pltpu.make_async_copy(state_bf, state_out, sems.at[heads + 1]),
    ]
    for copy in kept:
        copy.start()
    inverse, _ = position_factors(s0, s1, s2, s3)
    for h in range(heads):
        columns = slice(h * DH, (h + 1) * DH)
        rows[h] = (att[:, columns] * inverse * gain[:, columns]).astype(bf16)
        kept.append(pltpu.make_async_copy(rows.at[h], out.at[:, columns], sems.at[h]))
        kept[-1].start()
    for copy in kept:
        copy.wait()


def query_kernel(grad, k, v, state_bf, out):
    n = k.shape[0] // 2
    g, kh = grad[...], k[...]
    top, bottom = lower_scores(g, v[...], tri(n, False))
    far = nt(g, state_bf[...])
    out[:n, :] = (far[:n] + nn(top, kh[:n])).astype(bf16)
    out[n:, :] = (far[n:] + nn(bottom, kh)).astype(bf16)


def near_kernel(q, k, v, grad, key_near, value_near):
    n = k.shape[0] // 2
    mask = tri(n, True)
    g, qh = grad[...], q[...]
    top, bottom = upper_scores(v[...], g, mask)
    key_near[:n, :] = nn(top, qh)
    key_near[n:, :] = nn(bottom, qh[n:])
    top, bottom = upper_scores(k[...], qh, mask)
    value_near[:n, :] = nn(top, g)
    value_near[n:, :] = nn(bottom, g[n:])


def by_head(kernel, outs, *args):
    columns = args[0].shape[1]

    def spec(shape):
        if shape[1] == columns:
            return pl.BlockSpec((shape[0], DH), lambda h: (0, h))
        return pl.BlockSpec((DH, DH), lambda h: (h, 0))

    return pl.pallas_call(
        kernel,
        grid=(columns // DH,),
        out_shape=[pltpu.HBM(s, d) for s, d in outs],
        in_specs=[spec(x.shape) for x in args],
        out_specs=[spec(s) for s, _ in outs],
        compiler_params=pltpu.CompilerParams(vmem_limit_bytes=24 << 20),
    )(*[pltpu.with_memory_space_constraint(x, pltpu.HBM) for x in args])


def finish_kernel(own, k, v, key_near, value_near, suffix, recv, *rest):
    grad_key, grad_value, k_buf, v_buf, kn_buf, vn_buf, recv_buf, key_buf, value_buf, sems = rest[-10:]
    half = k_buf.shape[0]
    core = core_index()
    base = (core if own else 1 - core) * half
    rows = pl.ds(pl.multiple_of(base * DH, DH), half * DH)
    states = pltpu.make_async_copy(recv.at[rows, :], recv_buf, sems.at[6, 0])
    states.start()
    copies = fetch(
        (k, v, key_near, value_near), (k_buf, v_buf, kn_buf, vn_buf), sems,
        [base + i for i in range(half)],
    )
    states.wait()
    earlier = (core == 0).astype(f32)
    sent = []
    for i in range(half):
        at = slice(i * DH, (i + 1) * DH)
        state = (suffix[at, :] + earlier * recv_buf[at, :]).astype(bf16)
        for copy in copies[i]:
            copy.wait()
        key_buf[i] = (nt(v_buf[i], state) + kn_buf[i]).astype(bf16)
        value_buf[i] = (nn(k_buf[i], state) + vn_buf[i]).astype(bf16)
        for n, (buf, out) in enumerate(((key_buf, grad_key), (value_buf, grad_value))):
            sent.append(pltpu.make_async_copy(buf.at[i], out.at[:, col(base + i)], sems.at[4 + n, i]))
            sent[-1].start()
    for copy in sent:
        copy.wait()


def pack_kernel(states, recv, out):
    peers, rows, _ = out.shape
    count = peers * (rows - 8)
    half = pl.ds(pl.multiple_of(core_index() * count, count), count)
    near = states[half, :] + recv[half, :]
    out[:, : rows - 8, :] = near.reshape(peers, rows - 8, DH)
    gains = states[2 * count :, :] + recv[2 * count :, :]
    out[:, rows - 8 :, :] = jnp.broadcast_to(gains[None], (peers, 8, DH))


def body(query_rows, key_rows, value_rows, norm_gain, out_grad):
    q, k, v, do = query_rows, key_rows, value_rows, out_grad
    tokens, width = q.shape
    gain = norm_gain.reshape(1, width)
    peers = lax.axis_size("seq")
    chips = peers // 2
    ring = lax.axis_size("head")
    half = width // DH // 2
    state_rows = half * DH
    slice_rows = state_rows // chips
    swap_pairs = [(i, i ^ 1) for i in range(peers)]
    groups = [[2 * i + c for i in range(chips)] for c in range(2)]

    def swap(x):
        return lax.ppermute(x, "seq", swap_pairs)

    def exchange(x):
        return lax.all_to_all(x, "seq", 0, 0, axis_index_groups=groups)

    def scan(x, reverse):
        rows = x.shape[1] - slice_rows
        outs = [((chips, slice_rows, DH), f32)] + ([((rows, DH), f32)] if rows else [])
        kernel = lambda *refs: scan_kernel(reverse, slice_rows, *refs)
        return call(kernel, outs, x)

    slices = ((chips, slice_rows, DH), f32)
    wide = ((tokens, width), f32)
    narrow = ((tokens, width), bf16)
    heads = 2 * half

    def buffers(count, *kinds):
        return [pltpu.VMEM((count, tokens, DH), kind) for kind in kinds]

    (states,) = call(
        states_kernel, [((width, DH), f32)], k, v, ins=[HBM, HBM],
        scratch=buffers(heads, bf16, bf16) + [pltpu.SemaphoreType.DMA((2, heads))],
    )
    recv = swap(states)
    (near,) = call(add_kernel, [slices], states, recv)
    (before,) = scan(exchange(near), False)
    before = exchange(before).reshape(state_rows, DH)
    other = swap(before)
    (local,) = call(local_kernel, [wide], q, k, v)
    att, state_bf, stats = call(
        attend_kernel,
        [wide, ((width, DH), bf16), ((8, tokens), f32)],
        q, local, before, other, recv, do, gain,
    )
    parts = [stats] + [
        lax.ppermute(stats, "head", [(i, (i + d) % ring) for i in range(ring)])
        for d in range(1, ring)
    ]
    grad, states, _ = call(
        norm_kernel,
        [narrow, ((width + 8, DH), f32), ((1, width), f32)],
        q, att, do, gain, *parts,
    )
    recv = swap(states)
    attn_out, grad, state_bf = call(
        output_kernel, [narrow, narrow, ((width, DH), bf16)],
        att, gain, *parts, grad, state_bf, places=[HBM] * 3,
        scratch=buffers(heads, bf16) + [pltpu.SemaphoreType.DMA((heads + 2,))],
    )
    recv, attn_out = lax.optimization_barrier((recv, attn_out))
    (packed,) = call(pack_kernel, [((chips, slice_rows + 8, DH), f32)], states, recv)
    after, grad_gain = scan(exchange(packed), True)
    after, q2, k2, v2, grad = lax.optimization_barrier((after, q, k, v, grad))
    (grad_query,) = by_head(query_kernel, [narrow], grad, k2, v2, state_bf)
    key_near, value_near = by_head(near_kernel, [wide, wide], q2, k2, v2, grad)
    after, grad_query, key_near, value_near = lax.optimization_barrier(
        (exchange(after), grad_query, key_near, value_near)
    )
    after = after.reshape(state_rows, DH)
    other = swap(after)
    pair = [narrow, narrow]
    scratch = buffers(half, bf16, bf16, f32, f32) + [pltpu.VMEM((state_rows, DH), f32)]
    scratch += buffers(half, bf16, bf16) + [pltpu.SemaphoreType.DMA((7, half))]
    ins = [HBM] * 4 + [VMEM, HBM]
    own = call(
        functools.partial(finish_kernel, True), pair,
        k, v, key_near, value_near, after, recv,
        ins=ins, places=[HBM] * 2, scratch=scratch,
    )
    other, *own = lax.optimization_barrier((other, *own))
    grad_key, grad_value = call(
        functools.partial(finish_kernel, False), pair,
        k, v, key_near, value_near, other, recv, *own,
        ins=ins + [HBM] * 2, places=[HBM] * 2, scratch=scratch, aliases={6: 0, 7: 1},
    )
    return attn_out, grad_query, grad_key, grad_value, grad_gain.reshape(width)


def solution(mesh):
    rows, heads = P("seq", "head"), P("head")
    return jax.shard_map(
        body,
        mesh=mesh,
        in_specs=(rows, rows, rows, heads, rows),
        out_specs=(rows, rows, rows, rows, heads),
        check_vma=False,
    )
```

```python
import functools

import jax
import jax.numpy as jnp
from jax import lax
from jax.experimental import pallas as pl
from jax.experimental.pallas import tpu as pltpu
from jax.sharding import PartitionSpec as P

HEADS = 32
DH = 128
COLUMNS = HEADS * DH
EPS = 1e-06

f32 = jnp.float32
bf16 = jnp.bfloat16
VMEM = pl.BlockSpec(memory_space=pltpu.VMEM)
HBM = pl.BlockSpec(memory_space=pltpu.HBM)


def nn(a, b):
    return lax.dot_general(a, b, (((1,), (0,)), ((), ())), preferred_element_type=f32)


def nt(a, b):
    return lax.dot_general(a, b, (((1,), (1,)), ((), ())), preferred_element_type=f32)


def tn(a, b):
    return lax.dot_general(a, b, (((0,), (0,)), ((), ())), preferred_element_type=f32)


def call(kernel, outs, *args, ins=None, places=None, scratch=(), aliases={}):
    ins = ins or [VMEM] * len(args)
    places = places or [VMEM] * len(outs)
    shapes = [
        pltpu.HBM(s, d) if place is HBM else jax.ShapeDtypeStruct(s, d)
        for (s, d), place in zip(outs, places)
    ]
    args = [
        pltpu.with_memory_space_constraint(x, pltpu.HBM) if place is HBM else x
        for x, place in zip(args, ins)
    ]
    return pl.pallas_call(
        kernel,
        out_shape=shapes,
        in_specs=ins,
        out_specs=places,
        scratch_shapes=scratch,
        input_output_aliases=aliases,
        compiler_params=pltpu.CompilerParams(vmem_limit_bytes=24 << 20),
    )(*args)


def core_index():
    return lax.rem(lax.axis_index("seq"), 2)


def col(head):
    return pl.ds(pl.multiple_of(head * DH, DH), DH)


def tri(n, upper):
    row = lax.broadcasted_iota(jnp.int32, (n, n), 0)
    column = lax.broadcasted_iota(jnp.int32, (n, n), 1)
    return column >= row if upper else column <= row


def lower_scores(a, b, mask):
    n = a.shape[0] // 2
    top = jnp.where(mask, nt(a[:n], b[:n]), 0.0).astype(bf16)
    left = nt(a[n:], b[:n]).astype(bf16)
    right = jnp.where(mask, nt(a[n:], b[n:]), 0.0).astype(bf16)
    return top, jnp.concatenate([left, right], axis=1)


def upper_scores(a, b, mask):
    n = a.shape[0] // 2
    left = jnp.where(mask, nt(a[:n], b[:n]), 0.0).astype(bf16)
    right = nt(a[:n], b[n:]).astype(bf16)
    bottom = jnp.where(mask, nt(a[n:], b[n:]), 0.0).astype(bf16)
    return jnp.concatenate([left, right], axis=1), bottom


def head_rows(head):
    return pl.ds(pl.multiple_of(head * DH, DH), DH)


def states_kernel(k, v, out, k_kept, v_kept, sems):
    heads = k.shape[1] // DH
    copies = []
    for h in range(0, heads, 2):
        at = slice(h * DH, (h + 2) * DH)
        for n, (ref, kept) in enumerate(((k, k_kept), (v, v_kept))):
            copies.append(pltpu.make_async_copy(ref.at[:, at], kept.at[:, at], sems.at[n, h]))
            copies[-1].start()
    for h in range(heads):
        at = slice(h * DH, (h + 1) * DH)
        if h % 2 == 0:
            copies[h].wait()
            copies[h + 1].wait()
        out[at, :] = tn(k_kept[:, at], v_kept[:, at])


def add_kernel(states, recv, out):
    rows = out.shape[0] * out.shape[1]
    half = pl.ds(pl.multiple_of(core_index() * rows, rows), rows)
    out[...] = (states[half, :] + recv[half, :]).reshape(out.shape)


def local_kernel(first, q, k, v, out):
    heads = out.shape[1] // DH
    n = q.shape[0] // 2
    mask = tri(n, False)

    def step(h, _):
        top, bottom = lower_scores(q[:, col(first + h)], k[:, col(first + h)], mask)
        vh = v[:, col(first + h)]
        out[:n, col(h)] = nn(top, vh[:n])
        out[n:, col(h)] = nn(bottom, vh)
        return 0

    lax.fori_loop(0, heads, step, 0, unroll=2)


def turn_kernel(q, out):
    def step(h, _):
        out[head_rows(h), :] = q[:, col(h)].T
        return 0

    lax.fori_loop(0, q.shape[1] // DH, step, 0, unroll=2)


def scan_kernel(reverse, rows, x, out):
    peers = x.shape[0]

    run = jnp.zeros(out.shape[1:], f32)
    for at in range(peers - 1, -1, -1) if reverse else range(peers):
        out[at] = run
        run = run + x[at, :rows]


def attend_kernel(q, local_low, local_high, pre, other, recv, do, gain, att, state_bf, stats):
    half = q.shape[1] // DH // 2
    core = core_index()
    later = (core == 1).astype(f32)

    def step(i, sums):
        own, far = pre[head_rows(i), :], other[head_rows(i), :]
        low = jnp.where(core == 0, own, far)
        high = jnp.where(core == 0, far, own)
        squares, dots = sums
        for h, state, local in ((i, low, local_low), (i + half, high, local_high)):
            state = (state + later * recv[head_rows(h), :]).astype(bf16)
            state_bf[head_rows(h), :] = state
            a = local[:, col(i)] + nn(q[:, col(h)], state)
            att[:, col(h)] = a
            squares = squares + a * a
            dots = dots + (do[:, col(h)].astype(f32) * gain[:, col(h)]) * a
        return squares, dots

    zero = jnp.zeros((q.shape[0], DH), f32)
    squares, dots = lax.fori_loop(0, half, step, (zero, zero))
    stats[0:1, :] = jnp.sum(squares.T, axis=0, keepdims=True)
    stats[1:2, :] = jnp.sum(dots.T, axis=0, keepdims=True)
    stats[2:8, :] = jnp.zeros((6, q.shape[0]), f32)


def position_factors(s0, s1, s2, s3):
    sums = (s0[...] + s1[...] + s2[...] + s3[...]).T
    inverse = lax.rsqrt(sums[:, 0:1] / COLUMNS + EPS)
    mean = sums[:, 1:2] * inverse / COLUMNS
    shape = (sums.shape[0], DH)
    return jnp.broadcast_to(inverse, shape), jnp.broadcast_to(mean, shape)


def norm_kernel(turned, att, do, gain, s0, s1, s2, s3, grad, states, gains):
    heads = att.shape[1] // DH
    inverse, mean = position_factors(s0, s1, s2, s3)

    def step(h, _):
        wide = do[:, col(h)].astype(f32)
        normed = att[:, col(h)] * inverse
        gains[:, col(h)] = jnp.sum(wide * normed, axis=0, keepdims=True)
        g = (inverse * (wide * gain[:, col(h)] - normed * mean)).astype(bf16)
        grad[:, col(h)] = g
        states[head_rows(h), :] = nn(turned[head_rows(h), :], g)
        return 0

    lax.fori_loop(0, heads, step, 0, unroll=2)
    for h in range(heads):
        states[heads * DH + h : heads * DH + h + 1, :] = gains[:, h * DH : (h + 1) * DH]


def output_kernel(att, gain, s0, s1, s2, s3, grad, state_bf, out, grad_out, state_out, rows, sems):
    heads = att.shape[1] // DH
    kept = [
        pltpu.make_async_copy(grad, grad_out, sems.at[heads]),
        pltpu.make_async_copy(state_bf, state_out, sems.at[heads + 1]),
    ]
    for copy in kept:
        copy.start()
    inverse, _ = position_factors(s0, s1, s2, s3)
    for h in range(heads):
        columns = slice(h * DH, (h + 1) * DH)
        rows[h] = (att[:, columns] * inverse * gain[:, columns]).astype(bf16)
        kept.append(pltpu.make_async_copy(rows.at[h], out.at[:, columns], sems.at[h]))
        kept[-1].start()
    for copy in kept:
        copy.wait()


def grads_kernel(q, k, v, grad, state_bf, out, key_near, value_near):
    n = k.shape[0] // 2
    lower, upper = tri(n, False), tri(n, True)
    for h in range(k.shape[1] // DH):
        at = slice(h * DH, (h + 1) * DH)
        g, qh, kh, vh = grad[:, at], q[:, at], k[:, at], v[:, at]
        top, bottom = lower_scores(g, vh, lower)
        far = nt(g, state_bf[at, :])
        out[:n, at] = (far[:n] + nn(top, kh[:n])).astype(bf16)
        out[n:, at] = (far[n:] + nn(bottom, kh)).astype(bf16)
        top, bottom = upper_scores(vh, g, upper)
        key_near[:n, at] = nn(top, qh)
        key_near[n:, at] = nn(bottom, qh[n:])
        top, bottom = upper_scores(kh, qh, upper)
        value_near[:n, at] = nn(top, g)
        value_near[n:, at] = nn(bottom, g[n:])


def by_head(kernel, outs, *args):
    columns = args[0].shape[1]

    def spec(shape):
        if shape[1] == columns:
            return pl.BlockSpec((shape[0], 2 * DH), lambda h: (0, h))
        return pl.BlockSpec((2 * DH, DH), lambda h: (h, 0))

    return pl.pallas_call(
        kernel,
        grid=(columns // DH // 2,),
        out_shape=[pltpu.HBM(s, d) for s, d in outs],
        in_specs=[spec(x.shape) for x in args],
        out_specs=[spec(s) for s, _ in outs],
        compiler_params=pltpu.CompilerParams(vmem_limit_bytes=24 << 20),
    )(*[pltpu.with_memory_space_constraint(x, pltpu.HBM) for x in args])


def finish_head(h, state, k, v, key_near, value_near, outs, buffers, sems, slot):
    buffers[0][slot] = (nt(v[:, col(h)], state) + key_near).astype(bf16)
    buffers[1][slot] = (nn(k[:, col(h)], state) + value_near).astype(bf16)
    copies = [
        pltpu.make_async_copy(buffer.at[slot], out.at[:, col(h)], sems.at[n, slot])
        for n, (buffer, out) in enumerate(zip(buffers, outs))
    ]
    for copy in copies:
        copy.start()
    return copies


def finish_state(suffix, recv, i, h):
    earlier = (core_index() == 0).astype(f32)
    return (suffix[i * DH : (i + 1) * DH, :] + earlier * recv[head_rows(h), :]).astype(bf16)


def finish_own_kernel(
    k, v, key_near, value_near, suffix, recv, gathered,
    grad_key, grad_value, grad_gain, key_far, value_far,
    key_own, value_own, key_buf, value_buf, total, sems, out_sems,
):
    half = key_buf.shape[0]
    core = core_index()
    near = []
    for base, buffers in ((core, (key_own, value_own)), (1 - core, (key_far, value_far))):
        for i in range(half):
            near.append([
                pltpu.make_async_copy(
                    ref.at[:, col(base * half + i)], buffer.at[i], sems.at[n, len(near)]
                )
                for n, (ref, buffer) in enumerate(zip((key_near, value_near), buffers))
            ])
            for copy in near[-1]:
                copy.start()
    total[...] = jnp.sum(gathered[:, gathered.shape[1] - 8 :], axis=0)
    sent = [pltpu.make_async_copy(total, grad_gain, out_sems.at[2, 0])]
    sent[0].start()
    for i in range(half):
        h = core * half + i
        state = finish_state(suffix, recv, i, h)
        for copy in near[i]:
            copy.wait()
        sent += finish_head(
            h, state, k, v, key_own[i], value_own[i],
            (grad_key, grad_value), (key_buf, value_buf), out_sems, i,
        )
    for copy in sum(near[half:], sent):
        copy.wait()


def finish_far_kernel(
    k, v, key_far, value_far, suffix, recv, key_in, value_in,
    grad_key, grad_value, key_buf, value_buf, sems,
):
    half = key_buf.shape[0]
    sent = []
    for i in range(half):
        h = (1 - core_index()) * half + i
        sent += finish_head(
            h, finish_state(suffix, recv, i, h), k, v, key_far[i], value_far[i],
            (grad_key, grad_value), (key_buf, value_buf), sems, i,
        )
    for copy in sent:
        copy.wait()


def pack_kernel(states, recv, out, recv_out, buffer, sems):
    peers, rows, _ = out.shape
    count = peers * (rows - 8)
    keep = pltpu.make_async_copy(recv, recv_out, sems.at[0])
    gains = states[2 * count :, :] + recv[2 * count :, :]
    sent = []
    part = peers // 4
    for n in range(4):
        at = slice(n * part, (n + 1) * part)
        size = count // 4
        half = pl.ds(pl.multiple_of(core_index() * count + n * size, size), size)
        near = states[half, :] + recv[half, :]
        buffer[at, : rows - 8, :] = near.reshape(part, rows - 8, DH)
        buffer[at, rows - 8 :, :] = jnp.broadcast_to(gains[None], (part, 8, DH))
        sent.append(pltpu.make_async_copy(buffer.at[at], out.at[at], sems.at[1 + n]))
        sent[-1].start()
        if n == 0:
            keep.start()
    for copy in [keep] + sent:
        copy.wait()


def body(query_rows, key_rows, value_rows, norm_gain, out_grad):
    q, k, v, do = query_rows, key_rows, value_rows, out_grad
    tokens, width = q.shape
    gain = norm_gain.reshape(1, width)
    peers = lax.axis_size("seq")
    chips = peers // 2
    ring = lax.axis_size("head")
    half = width // DH // 2
    state_rows = half * DH
    slice_rows = state_rows // chips
    swap_pairs = [(i, i ^ 1) for i in range(peers)]
    groups = [[2 * i + c for i in range(chips)] for c in range(2)]

    def swap(x):
        return lax.ppermute(x, "seq", swap_pairs)

    def exchange(x):
        return lax.all_to_all(x, "seq", 0, 0, axis_index_groups=groups)

    def scan(x, reverse):
        kernel = functools.partial(scan_kernel, reverse, slice_rows)
        return call(kernel, [((chips, slice_rows, DH), f32)], x)

    slices = ((chips, slice_rows, DH), f32)
    wide = ((tokens, width), f32)
    narrow = ((tokens, width), bf16)
    heads = 2 * half

    def buffers(count, *kinds):
        return [pltpu.VMEM((count, tokens, DH), kind) for kind in kinds]

    states, k_kept, v_kept = call(
        states_kernel, [((width, DH), f32), narrow, narrow], k, v, ins=[HBM, HBM],
        scratch=[pltpu.SemaphoreType.DMA((2, heads))],
    )
    recv = swap(states)
    local = [((tokens, width // 2), f32)]
    (low,) = call(functools.partial(local_kernel, 0), local, q, k_kept, v_kept)
    recv, low, q1 = lax.optimization_barrier((recv, low, q))
    (near,) = call(add_kernel, [slices], states, recv)
    (before,) = scan(exchange(near), False)
    before, q1, k1, v1 = lax.optimization_barrier((exchange(before), q, k_kept, v_kept))
    before = before.reshape(state_rows, DH)
    other = swap(before)
    (high,) = call(functools.partial(local_kernel, half), local, q1, k1, v1)
    att, state_bf, stats = call(
        attend_kernel,
        [wide, ((width, DH), bf16), ((8, tokens), f32)],
        q, low, high, before, other, recv, do, gain,
    )
    parts = [
        lax.ppermute(stats, "head", [(i, (i + d) % ring) for i in range(ring)])
        for d in (1, 3, 2)[: ring - 1]
    ]
    q1, stats = lax.optimization_barrier((q, stats))
    (turned,) = call(turn_kernel, [((width, tokens), bf16)], q1)
    parts.append(stats)
    grad, states = call(
        norm_kernel,
        [narrow, ((width + 8, DH), f32)],
        turned, att, do, gain, *parts, scratch=[pltpu.VMEM((1, width), f32)],
    )
    recv = swap(states)
    attn_out, grad, state_bf = call(
        output_kernel, [narrow, narrow, ((width, DH), bf16)],
        att, gain, *parts, grad, state_bf, places=[HBM] * 3,
        scratch=buffers(heads, bf16) + [pltpu.SemaphoreType.DMA((heads + 2,))],
    )
    recv, attn_out = lax.optimization_barrier((recv, attn_out))
    packed = ((chips, slice_rows + 8, DH), f32)
    packed, recv = call(
        pack_kernel, [packed, ((width + 8, DH), f32)], states, recv, places=[HBM] * 2,
        scratch=[pltpu.VMEM(packed[0], f32), pltpu.SemaphoreType.DMA((5,))],
    )
    packed, recv, q2, k2, v2, grad = lax.optimization_barrier((packed, recv, q, k, v, grad))
    grad_query, key_near, value_near = by_head(
        grads_kernel, [narrow, wide, wide], q2, k2, v2, grad, state_bf
    )
    after, grad_query, key_near, value_near = lax.optimization_barrier(
        (exchange(packed), grad_query, key_near, value_near)
    )
    gathered = after
    (after,) = scan(gathered, True)
    after = exchange(after).reshape(state_rows, DH)
    other = swap(after)
    far = ((half, tokens, DH), f32)
    out_buffers = buffers(half, bf16, bf16)
    grad_key, grad_value, grad_gain, key_far, value_far = call(
        finish_own_kernel, [narrow, narrow, ((8, DH), f32), far, far],
        k2, v2, key_near, value_near, after, recv, gathered,
        ins=[VMEM] * 2 + [HBM] * 2 + [VMEM] * 3, places=[HBM] * 3 + [VMEM] * 2,
        scratch=buffers(half, f32, f32) + out_buffers + [
            pltpu.VMEM((8, DH), f32),
            pltpu.SemaphoreType.DMA((2, heads)), pltpu.SemaphoreType.DMA((3, half)),
        ],
    )
    other, key_far, value_far = lax.optimization_barrier((other, key_far, value_far))
    grad_key, grad_value = call(
        finish_far_kernel, [narrow, narrow],
        k2, v2, key_far, value_far, other, recv, grad_key, grad_value,
        ins=[VMEM] * 6 + [HBM] * 2, places=[HBM] * 2,
        scratch=out_buffers + [pltpu.SemaphoreType.DMA((2, half))], aliases={6: 0, 7: 1},
    )
    return attn_out, grad_query, grad_key, grad_value, grad_gain.reshape(width)


def solution(mesh):
    rows, heads = P("seq", "head"), P("head")
    return jax.shard_map(
        body,
        mesh=mesh,
        in_specs=(rows, rows, rows, heads, rows),
        out_specs=(rows, rows, rows, rows, heads),
        check_vma=False,
    )
```

```python
import functools

import jax
import jax.numpy as jnp
from jax import lax
from jax.experimental import pallas as pl
from jax.experimental.pallas import tpu as pltpu
from jax.sharding import PartitionSpec as P

HEADS = 32
DH = 128
COLUMNS = HEADS * DH
EPS = 1e-06

f32 = jnp.float32
bf16 = jnp.bfloat16
VMEM = pl.BlockSpec(memory_space=pltpu.VMEM)
HBM = pl.BlockSpec(memory_space=pltpu.HBM)


def nn(a, b):
    return lax.dot_general(a, b, (((1,), (0,)), ((), ())), preferred_element_type=f32)


def nt(a, b):
    return lax.dot_general(a, b, (((1,), (1,)), ((), ())), preferred_element_type=f32)


def tn(a, b):
    return lax.dot_general(a, b, (((0,), (0,)), ((), ())), preferred_element_type=f32)


def call(kernel, outs, *args, ins=None, places=None, scratch=(), aliases={}):
    ins = ins or [VMEM] * len(args)
    places = places or [VMEM] * len(outs)
    shapes = [
        pltpu.HBM(s, d) if place is HBM else jax.ShapeDtypeStruct(s, d)
        for (s, d), place in zip(outs, places)
    ]
    args = [
        pltpu.with_memory_space_constraint(x, pltpu.HBM) if place is HBM else x
        for x, place in zip(args, ins)
    ]
    return pl.pallas_call(
        kernel,
        out_shape=shapes,
        in_specs=ins,
        out_specs=places,
        scratch_shapes=scratch,
        input_output_aliases=aliases,
        compiler_params=pltpu.CompilerParams(vmem_limit_bytes=24 << 20),
    )(*args)


def core_index():
    return lax.rem(lax.axis_index("seq"), 2)


def col(head):
    return pl.ds(pl.multiple_of(head * DH, DH), DH)


def tri(n, upper):
    row = lax.broadcasted_iota(jnp.int32, (n, n), 0)
    column = lax.broadcasted_iota(jnp.int32, (n, n), 1)
    return column >= row if upper else column <= row


def lower_scores(a, b, mask):
    n = a.shape[0] // 2
    top = jnp.where(mask, nt(a[:n], b[:n]), 0.0).astype(bf16)
    left = nt(a[n:], b[:n]).astype(bf16)
    right = jnp.where(mask, nt(a[n:], b[n:]), 0.0).astype(bf16)
    return top, jnp.concatenate([left, right], axis=1)


def upper_scores(a, b, mask):
    n = a.shape[0] // 2
    left = jnp.where(mask, nt(a[:n], b[:n]), 0.0).astype(bf16)
    right = nt(a[:n], b[n:]).astype(bf16)
    bottom = jnp.where(mask, nt(a[n:], b[n:]), 0.0).astype(bf16)
    return jnp.concatenate([left, right], axis=1), bottom


def head_rows(head):
    return pl.ds(pl.multiple_of(head * DH, DH), DH)


def states_kernel(k, v, out, k_kept, v_kept, sems):
    heads = k.shape[1] // DH
    copies = []
    firsts = [0, 1] + list(range(2, heads, 2))
    for h, end in zip(firsts, firsts[1:] + [heads]):
        at = slice(h * DH, end * DH)
        for n, (ref, kept) in enumerate(((k, k_kept), (v, v_kept))):
            copies.append(pltpu.make_async_copy(ref.at[:, at], kept.at[:, at], sems.at[n, h]))
            copies[-1].start()
    for h in range(heads):
        at = slice(h * DH, (h + 1) * DH)
        if h in firsts:
            copies.pop(0).wait()
            copies.pop(0).wait()
        out[at, :] = tn(k_kept[:, at], v_kept[:, at])


def add_kernel(states, recv, out):
    rows = out.shape[0] * out.shape[1]
    half = pl.ds(pl.multiple_of(core_index() * rows, rows), rows)
    out[...] = (states[half, :] + recv[half, :]).reshape(out.shape)


def local_kernel(first, q, k, v, out):
    heads = out.shape[1] // DH
    n = q.shape[0] // 2
    mask = tri(n, False)

    def step(h, _):
        top, bottom = lower_scores(q[:, col(first + h)], k[:, col(first + h)], mask)
        vh = v[:, col(first + h)]
        out[:n, col(h)] = nn(top, vh[:n])
        out[n:, col(h)] = nn(bottom, vh)
        return 0

    lax.fori_loop(0, heads, step, 0, unroll=2)


def turn_kernel(q, out):
    def step(h, _):
        out[head_rows(h), :] = q[:, col(h)].T
        return 0

    lax.fori_loop(0, q.shape[1] // DH, step, 0, unroll=2)


def scan_kernel(reverse, rows, x, out):
    peers = x.shape[0]

    run = jnp.zeros(out.shape[1:], f32)
    for at in range(peers - 1, -1, -1) if reverse else range(peers):
        out[at] = run
        run = run + x[at, :rows]


def attend_kernel(q, local_low, local_high, pre, other, recv, do, gain, att, state_bf, stats):
    half = q.shape[1] // DH // 2
    core = core_index()
    later = (core == 1).astype(f32)

    def step(i, sums):
        own, far = pre[head_rows(i), :], other[head_rows(i), :]
        low = jnp.where(core == 0, own, far)
        high = jnp.where(core == 0, far, own)
        squares, dots = sums
        for h, state, local in ((i, low, local_low), (i + half, high, local_high)):
            state = (state + later * recv[head_rows(h), :]).astype(bf16)
            state_bf[head_rows(h), :] = state
            a = local[:, col(i)] + nn(q[:, col(h)], state)
            att[:, col(h)] = a
            squares = squares + a * a
            dots = dots + (do[:, col(h)].astype(f32) * gain[:, col(h)]) * a
        return squares, dots

    zero = jnp.zeros((q.shape[0], DH), f32)
    squares, dots = lax.fori_loop(0, half, step, (zero, zero), unroll=2)
    stats[0:1, :] = jnp.sum(squares.T, axis=0, keepdims=True)
    stats[1:2, :] = jnp.sum(dots.T, axis=0, keepdims=True)
    stats[2:8, :] = jnp.zeros((6, q.shape[0]), f32)


def position_factors(s0, s1, s2, s3):
    sums = (s0[...] + s1[...] + s2[...] + s3[...]).T
    inverse = lax.rsqrt(sums[:, 0:1] / COLUMNS + EPS)
    mean = sums[:, 1:2] * inverse / COLUMNS
    shape = (sums.shape[0], DH)
    return jnp.broadcast_to(inverse, shape), jnp.broadcast_to(mean, shape)


def norm_kernel(turned, att, do, gain, s0, s1, s2, s3, grad, states, gains):
    heads = att.shape[1] // DH
    inverse, mean = position_factors(s0, s1, s2, s3)

    def step(h, _):
        wide = do[:, col(h)].astype(f32)
        normed = att[:, col(h)] * inverse
        gains[:, col(h)] = jnp.sum(wide * normed, axis=0, keepdims=True)
        g = (inverse * (wide * gain[:, col(h)] - normed * mean)).astype(bf16)
        grad[:, col(h)] = g
        states[head_rows(h), :] = nn(turned[head_rows(h), :], g)
        return 0

    lax.fori_loop(0, heads, step, 0, unroll=4)
    for h in range(heads):
        states[heads * DH + h : heads * DH + h + 1, :] = gains[:, h * DH : (h + 1) * DH]


def output_kernel(att, gain, s0, s1, s2, s3, grad, state_bf, out, grad_out, state_out, rows, sems):
    heads = att.shape[1] // DH
    kept = [
        pltpu.make_async_copy(grad, grad_out, sems.at[heads]),
        pltpu.make_async_copy(state_bf, state_out, sems.at[heads + 1]),
    ]
    for copy in kept:
        copy.start()
    inverse, _ = position_factors(s0, s1, s2, s3)
    for h in range(heads):
        columns = slice(h * DH, (h + 1) * DH)
        rows[h] = (att[:, columns] * inverse * gain[:, columns]).astype(bf16)
        kept.append(pltpu.make_async_copy(rows.at[h], out.at[:, columns], sems.at[h]))
        kept[-1].start()
    for copy in kept:
        copy.wait()


def grads_kernel(q, k, v, grad, state_bf, out, key_near, value_near):
    n = k.shape[0] // 2
    lower, upper = tri(n, False), tri(n, True)
    for h in range(k.shape[1] // DH):
        at = slice(h * DH, (h + 1) * DH)
        g, qh, kh, vh = grad[:, at], q[:, at], k[:, at], v[:, at]
        top, bottom = lower_scores(g, vh, lower)
        far = nt(g, state_bf[at, :])
        out[:n, at] = (far[:n] + nn(top, kh[:n])).astype(bf16)
        out[n:, at] = (far[n:] + nn(bottom, kh)).astype(bf16)
        top, bottom = upper_scores(vh, g, upper)
        key_near[:n, at] = nn(top, qh)
        key_near[n:, at] = nn(bottom, qh[n:])
        top, bottom = upper_scores(kh, qh, upper)
        value_near[:n, at] = nn(top, g)
        value_near[n:, at] = nn(bottom, g[n:])


def by_head(kernel, outs, *args):
    columns = args[0].shape[1]

    def spec(shape):
        if shape[1] == columns:
            return pl.BlockSpec((shape[0], 2 * DH), lambda h: (0, h))
        return pl.BlockSpec((2 * DH, DH), lambda h: (h, 0))

    return pl.pallas_call(
        kernel,
        grid=(columns // DH // 2,),
        out_shape=[pltpu.HBM(s, d) for s, d in outs],
        in_specs=[spec(x.shape) for x in args],
        out_specs=[spec(s) for s, _ in outs],
        compiler_params=pltpu.CompilerParams(vmem_limit_bytes=24 << 20),
    )(*[pltpu.with_memory_space_constraint(x, pltpu.HBM) for x in args])


def finish_head(h, state, k, v, key_near, value_near, key_out, value_out, slot):
    key_out[slot] = (nt(v[:, col(h)], state) + key_near).astype(bf16)
    value_out[slot] = (nn(k[:, col(h)], state) + value_near).astype(bf16)


def copy_heads(base, count, slots, outs, sems, first):
    copies = [
        pltpu.make_async_copy(buffer.at[i], out.at[:, col(base + i)], sems.at[n, first + i])
        for i in range(count)
        for n, (buffer, out) in enumerate(zip(slots, outs))
    ]
    for copy in copies:
        copy.start()
    return copies


def finish_state(suffix, recv, i, h):
    earlier = (core_index() == 0).astype(f32)
    return (suffix[i * DH : (i + 1) * DH, :] + earlier * recv[head_rows(h), :]).astype(bf16)


def finish_own_kernel(
    k, v, key_near, value_near, suffix, recv, gathered,
    grad_gain, key_done, value_done, key_far, value_far,
    key_own, value_own, total, sems, gain_sem,
):
    half = key_done.shape[0]
    core = core_index()
    near = []
    for base, buffers in ((core, (key_own, value_own)), (1 - core, (key_far, value_far))):
        for i in range(half):
            near.append([
                pltpu.make_async_copy(
                    ref.at[:, col(base * half + i)], buffer.at[i], sems.at[n, len(near)]
                )
                for n, (ref, buffer) in enumerate(zip((key_near, value_near), buffers))
            ])
            for copy in near[-1]:
                copy.start()
    total[...] = jnp.sum(gathered[:, gathered.shape[1] - 8 :], axis=0)
    gain = pltpu.make_async_copy(total, grad_gain, gain_sem)
    gain.start()
    for i in range(half):
        h = core * half + i
        state = finish_state(suffix, recv, i, h)
        for copy in near[i]:
            copy.wait()
        finish_head(h, state, k, v, key_own[i], value_own[i], key_done, value_done, i)
    for copy in sum(near[half:], [gain]):
        copy.wait()


def finish_far_kernel(
    k, v, key_far, value_far, suffix, recv, key_done, value_done,
    grad_key, grad_value, key_buf, value_buf, sems,
):
    half = key_buf.shape[0]
    core = core_index()
    outs = (grad_key, grad_value)
    sent = copy_heads(core * half, half, (key_done, value_done), outs, sems, 0)
    for i in range(half):
        h = (1 - core) * half + i
        state = finish_state(suffix, recv, i, h)
        finish_head(h, state, k, v, key_far[i], value_far[i], key_buf, value_buf, i)
        slots = (key_buf.at[pl.ds(i, 1)], value_buf.at[pl.ds(i, 1)])
        sent += copy_heads(h, 1, slots, outs, sems, half + i)
    for copy in sent:
        copy.wait()


def pack_kernel(states, recv, out, recv_out, buffer, sems):
    peers, rows, _ = out.shape
    count = peers * (rows - 8)
    keep = pltpu.make_async_copy(recv, recv_out, sems.at[0])
    gains = states[2 * count :, :] + recv[2 * count :, :]
    sent = []
    part = peers // 4
    for n in range(4):
        at = slice(n * part, (n + 1) * part)
        size = count // 4
        half = pl.ds(pl.multiple_of(core_index() * count + n * size, size), size)
        near = states[half, :] + recv[half, :]
        buffer[at, : rows - 8, :] = near.reshape(part, rows - 8, DH)
        buffer[at, rows - 8 :, :] = jnp.broadcast_to(gains[None], (part, 8, DH))
        sent.append(pltpu.make_async_copy(buffer.at[at], out.at[at], sems.at[1 + n]))
        sent[-1].start()
        if n == 0:
            keep.start()
    for copy in [keep] + sent:
        copy.wait()


def body(query_rows, key_rows, value_rows, norm_gain, out_grad):
    q, k, v, do = query_rows, key_rows, value_rows, out_grad
    tokens, width = q.shape
    gain = norm_gain.reshape(1, width)
    peers = lax.axis_size("seq")
    chips = peers // 2
    ring = lax.axis_size("head")
    half = width // DH // 2
    state_rows = half * DH
    slice_rows = state_rows // chips
    swap_pairs = [(i, i ^ 1) for i in range(peers)]
    groups = [[2 * i + c for i in range(chips)] for c in range(2)]

    def swap(x):
        return lax.ppermute(x, "seq", swap_pairs)

    def exchange(x):
        return lax.all_to_all(x, "seq", 0, 0, axis_index_groups=groups)

    def scan(x, reverse):
        kernel = functools.partial(scan_kernel, reverse, slice_rows)
        return call(kernel, [((chips, slice_rows, DH), f32)], x)

    slices = ((chips, slice_rows, DH), f32)
    wide = ((tokens, width), f32)
    narrow = ((tokens, width), bf16)
    heads = 2 * half

    def buffers(count, *kinds):
        return [pltpu.VMEM((count, tokens, DH), kind) for kind in kinds]

    states, k_kept, v_kept = call(
        states_kernel, [((width, DH), f32), narrow, narrow], k, v, ins=[HBM, HBM],
        scratch=[pltpu.SemaphoreType.DMA((2, heads))],
    )
    recv = swap(states)
    local = [((tokens, width // 2), f32)]
    (low,) = call(functools.partial(local_kernel, 0), local, q, k_kept, v_kept)
    recv, low, q1 = lax.optimization_barrier((recv, low, q))
    (near,) = call(add_kernel, [slices], states, recv)
    (before,) = scan(exchange(near), False)
    before, q1, k1, v1 = lax.optimization_barrier((exchange(before), q, k_kept, v_kept))
    before = before.reshape(state_rows, DH)
    other = swap(before)
    (high,) = call(functools.partial(local_kernel, half), local, q1, k1, v1)
    att, state_bf, stats = call(
        attend_kernel,
        [wide, ((width, DH), bf16), ((8, tokens), f32)],
        q, low, high, before, other, recv, do, gain,
    )
    parts = [
        lax.ppermute(stats, "head", [(i, (i + d) % ring) for i in range(ring)])
        for d in (1, 3, 2)[: ring - 1]
    ]
    q1, stats = lax.optimization_barrier((q, stats))
    (turned,) = call(turn_kernel, [((width, tokens), bf16)], q1)
    parts.append(stats)
    grad, states = call(
        norm_kernel,
        [narrow, ((width + 8, DH), f32)],
        turned, att, do, gain, *parts, scratch=[pltpu.VMEM((1, width), f32)],
    )
    recv = swap(states)
    attn_out, grad, state_bf = call(
        output_kernel, [narrow, narrow, ((width, DH), bf16)],
        att, gain, *parts, grad, state_bf, places=[HBM] * 3,
        scratch=buffers(heads, bf16) + [pltpu.SemaphoreType.DMA((heads + 2,))],
    )
    recv, attn_out = lax.optimization_barrier((recv, attn_out))
    packed = ((chips, slice_rows + 8, DH), f32)
    packed, recv = call(
        pack_kernel, [packed, ((width + 8, DH), f32)], states, recv, places=[HBM] * 2,
        scratch=[pltpu.VMEM(packed[0], f32), pltpu.SemaphoreType.DMA((5,))],
    )
    packed, recv, q2, k2, v2, grad = lax.optimization_barrier((packed, recv, q, k, v, grad))
    grad_query, key_near, value_near = by_head(
        grads_kernel, [narrow, wide, wide], q2, k2, v2, grad, state_bf
    )
    after, grad_query, key_near, value_near = lax.optimization_barrier(
        (exchange(packed), grad_query, key_near, value_near)
    )
    gathered = after
    (after,) = scan(gathered, True)
    after = exchange(after).reshape(state_rows, DH)
    other = swap(after)
    far = ((half, tokens, DH), f32)
    done = ((half, tokens, DH), bf16)
    grad_gain, key_done, value_done, key_far, value_far = call(
        finish_own_kernel, [((8, DH), f32), done, done, far, far],
        k2, v2, key_near, value_near, after, recv, gathered,
        ins=[VMEM] * 2 + [HBM] * 2 + [VMEM] * 3, places=[HBM] + [VMEM] * 4,
        scratch=buffers(half, f32, f32) + [
            pltpu.VMEM((8, DH), f32),
            pltpu.SemaphoreType.DMA((2, heads)), pltpu.SemaphoreType.DMA,
        ],
    )
    other, key_far, value_far = lax.optimization_barrier((other, key_far, value_far))
    grad_key, grad_value = call(
        finish_far_kernel, [narrow, narrow],
        k2, v2, key_far, value_far, other, recv, key_done, value_done,
        places=[HBM] * 2,
        scratch=buffers(half, bf16, bf16) + [pltpu.SemaphoreType.DMA((2, heads))],
    )
    return attn_out, grad_query, grad_key, grad_value, grad_gain.reshape(width)


def solution(mesh):
    rows, heads = P("seq", "head"), P("head")
    return jax.shard_map(
        body,
        mesh=mesh,
        in_specs=(rows, rows, rows, heads, rows),
        out_specs=(rows, rows, rows, rows, heads),
        check_vma=False,
    )
```

```python
import functools

import jax
import jax.numpy as jnp
from jax import lax
from jax.experimental import pallas as pl
from jax.experimental.pallas import tpu as pltpu
from jax.sharding import PartitionSpec as P

HEADS = 32
DH = 128
COLUMNS = HEADS * DH
EPS = 1e-06

f32 = jnp.float32
bf16 = jnp.bfloat16
VMEM = pl.BlockSpec(memory_space=pltpu.VMEM)
HBM = pl.BlockSpec(memory_space=pltpu.HBM)


def nn(a, b):
    return lax.dot_general(a, b, (((1,), (0,)), ((), ())), preferred_element_type=f32)


def nt(a, b):
    return lax.dot_general(a, b, (((1,), (1,)), ((), ())), preferred_element_type=f32)


def tn(a, b):
    return lax.dot_general(a, b, (((0,), (0,)), ((), ())), preferred_element_type=f32)


def call(kernel, outs, *args, ins=None, places=None, scratch=(), aliases={}):
    ins = ins or [VMEM] * len(args)
    places = places or [VMEM] * len(outs)
    shapes = [
        pltpu.HBM(s, d) if place is HBM else jax.ShapeDtypeStruct(s, d)
        for (s, d), place in zip(outs, places)
    ]
    args = [
        pltpu.with_memory_space_constraint(x, pltpu.HBM) if place is HBM else x
        for x, place in zip(args, ins)
    ]
    return pl.pallas_call(
        kernel,
        out_shape=shapes,
        in_specs=ins,
        out_specs=places,
        scratch_shapes=scratch,
        input_output_aliases=aliases,
        compiler_params=pltpu.CompilerParams(vmem_limit_bytes=24 << 20),
    )(*args)


def core_index():
    return lax.rem(lax.axis_index("seq"), 2)


def col(head):
    return pl.ds(pl.multiple_of(head * DH, DH), DH)


def tri(n, upper):
    row = lax.broadcasted_iota(jnp.int32, (n, n), 0)
    column = lax.broadcasted_iota(jnp.int32, (n, n), 1)
    return column >= row if upper else column <= row


def lower_scores(a, b, mask):
    n = a.shape[0] // 2
    top = jnp.where(mask, nt(a[:n], b[:n]), 0.0).astype(bf16)
    left = nt(a[n:], b[:n]).astype(bf16)
    right = jnp.where(mask, nt(a[n:], b[n:]), 0.0).astype(bf16)
    return top, jnp.concatenate([left, right], axis=1)


def upper_scores(a, b, mask):
    n = a.shape[0] // 2
    left = jnp.where(mask, nt(a[:n], b[:n]), 0.0).astype(bf16)
    right = nt(a[:n], b[n:]).astype(bf16)
    bottom = jnp.where(mask, nt(a[n:], b[n:]), 0.0).astype(bf16)
    return jnp.concatenate([left, right], axis=1), bottom


def head_rows(head):
    return pl.ds(pl.multiple_of(head * DH, DH), DH)


def states_kernel(k, v, out, k_kept, v_kept, sems):
    heads = k.shape[1] // DH
    copies = []
    firsts = list(range(0, heads, 2))
    for h, end in zip(firsts, firsts[1:] + [heads]):
        at = slice(h * DH, end * DH)
        for n, (ref, kept) in enumerate(((k, k_kept), (v, v_kept))):
            copies.append(pltpu.make_async_copy(ref.at[:, at], kept.at[:, at], sems.at[n, h]))
            copies[-1].start()
    for h in range(heads):
        at = slice(h * DH, (h + 1) * DH)
        if h in firsts:
            copies.pop(0).wait()
            copies.pop(0).wait()
        out[at, :] = tn(k_kept[:, at], v_kept[:, at])


def add_kernel(states, recv, out):
    rows = out.shape[0] * out.shape[1]
    half = pl.ds(pl.multiple_of(core_index() * rows, rows), rows)
    out[...] = (states[half, :] + recv[half, :]).reshape(out.shape)


def local_kernel(first, q, k, v, out):
    heads = out.shape[1] // DH
    n = q.shape[0] // 2
    mask = tri(n, False)

    def step(h, _):
        top, bottom = lower_scores(q[:, col(first + h)], k[:, col(first + h)], mask)
        vh = v[:, col(first + h)]
        out[:n, col(h)] = nn(top, vh[:n])
        out[n:, col(h)] = nn(bottom, vh)
        return 0

    lax.fori_loop(0, heads, step, 0, unroll=2)


def turn_kernel(q, out):
    def step(h, _):
        out[head_rows(h), :] = q[:, col(h)].T
        return 0

    lax.fori_loop(0, q.shape[1] // DH, step, 0, unroll=2)


def scan_kernel(reverse, rows, x, out):
    peers = x.shape[0]

    run = jnp.zeros(out.shape[1:], f32)
    for at in range(peers - 1, -1, -1) if reverse else range(peers):
        out[at] = run
        run = run + x[at, :rows]


def attend_kernel(q, local_low, local_high, pre, other, recv, do, gain, att, state_bf, stats):
    half = q.shape[1] // DH // 2
    core = core_index()
    later = (core == 1).astype(f32)

    def step(i, sums):
        own, far = pre[head_rows(i), :], other[head_rows(i), :]
        low = jnp.where(core == 0, own, far)
        high = jnp.where(core == 0, far, own)
        squares, dots = sums
        for h, state, local in ((i, low, local_low), (i + half, high, local_high)):
            state = (state + later * recv[head_rows(h), :]).astype(bf16)
            state_bf[head_rows(h), :] = state
            a = local[:, col(i)] + nn(q[:, col(h)], state)
            att[:, col(h)] = a
            squares = squares + a * a
            dots = dots + (do[:, col(h)].astype(f32) * gain[:, col(h)]) * a
        return squares, dots

    zero = jnp.zeros((q.shape[0], DH), f32)
    squares, dots = lax.fori_loop(0, half, step, (zero, zero), unroll=4)
    stats[0:1, :] = jnp.sum(squares.T, axis=0, keepdims=True)
    stats[1:2, :] = jnp.sum(dots.T, axis=0, keepdims=True)
    stats[2:8, :] = jnp.zeros((6, q.shape[0]), f32)


def position_factors(s0, s1, s2, s3):
    sums = (s0[...] + s1[...] + s2[...] + s3[...]).T
    inverse = lax.rsqrt(sums[:, 0:1] / COLUMNS + EPS)
    mean = sums[:, 1:2] * inverse / COLUMNS
    shape = (sums.shape[0], DH)
    return jnp.broadcast_to(inverse, shape), jnp.broadcast_to(mean, shape)


def norm_kernel(turned, att, do, gain, s0, s1, s2, s3, grad, states, gains):
    heads = att.shape[1] // DH
    inverse, mean = position_factors(s0, s1, s2, s3)

    def step(h, _):
        wide = do[:, col(h)].astype(f32)
        normed = att[:, col(h)] * inverse
        gains[:, col(h)] = jnp.sum(wide * normed, axis=0, keepdims=True)
        g = (inverse * (wide * gain[:, col(h)] - normed * mean)).astype(bf16)
        grad[:, col(h)] = g
        states[head_rows(h), :] = nn(turned[head_rows(h), :], g)
        return 0

    lax.fori_loop(0, heads, step, 0, unroll=8)
    for h in range(heads):
        states[heads * DH + h : heads * DH + h + 1, :] = gains[:, h * DH : (h + 1) * DH]


def output_kernel(att, gain, s0, s1, s2, s3, grad, state_bf, out, grad_out, state_out, rows, sems):
    heads = att.shape[1] // DH
    kept = [
        pltpu.make_async_copy(grad, grad_out, sems.at[heads]),
        pltpu.make_async_copy(state_bf, state_out, sems.at[heads + 1]),
    ]
    for copy in kept:
        copy.start()
    inverse, _ = position_factors(s0, s1, s2, s3)
    for h in range(heads):
        columns = slice(h * DH, (h + 1) * DH)
        rows[h] = (att[:, columns] * inverse * gain[:, columns]).astype(bf16)
        kept.append(pltpu.make_async_copy(rows.at[h], out.at[:, columns], sems.at[h]))
        kept[-1].start()
    for copy in kept:
        copy.wait()


def grads_kernel(q, k, v, grad, state_bf, out, key_near, value_near):
    n = k.shape[0] // 2
    lower, upper = tri(n, False), tri(n, True)
    for h in range(k.shape[1] // DH):
        at = slice(h * DH, (h + 1) * DH)
        g, qh, kh, vh = grad[:, at], q[:, at], k[:, at], v[:, at]
        top, bottom = lower_scores(g, vh, lower)
        far = nt(g, state_bf[at, :])
        out[:n, at] = (far[:n] + nn(top, kh[:n])).astype(bf16)
        out[n:, at] = (far[n:] + nn(bottom, kh)).astype(bf16)
        top, bottom = upper_scores(vh, g, upper)
        key_near[:n, at] = nn(top, qh)
        key_near[n:, at] = nn(bottom, qh[n:])
        top, bottom = upper_scores(kh, qh, upper)
        value_near[:n, at] = nn(top, g)
        value_near[n:, at] = nn(bottom, g[n:])


def by_head(kernel, outs, *args):
    columns = args[0].shape[1]

    def spec(shape):
        if shape[1] == columns:
            return pl.BlockSpec((shape[0], 2 * DH), lambda h: (0, h))
        return pl.BlockSpec((2 * DH, DH), lambda h: (h, 0))

    return pl.pallas_call(
        kernel,
        grid=(columns // DH // 2,),
        out_shape=[pltpu.HBM(s, d) for s, d in outs],
        in_specs=[spec(x.shape) for x in args],
        out_specs=[spec(s) for s, _ in outs],
        compiler_params=pltpu.CompilerParams(vmem_limit_bytes=24 << 20),
    )(*[pltpu.with_memory_space_constraint(x, pltpu.HBM) for x in args])


def finish_head(h, state, k, v, key_near, value_near, key_out, value_out, slot):
    key_out[slot] = (nt(v[:, col(h)], state) + key_near).astype(bf16)
    value_out[slot] = (nn(k[:, col(h)], state) + value_near).astype(bf16)


def copy_heads(base, count, slots, outs, sems, first):
    copies = [
        pltpu.make_async_copy(buffer.at[i], out.at[:, col(base + i)], sems.at[n, first + i])
        for i in range(count)
        for n, (buffer, out) in enumerate(zip(slots, outs))
    ]
    for copy in copies:
        copy.start()
    return copies


def finish_state(suffix, recv, i, h):
    earlier = (core_index() == 0).astype(f32)
    return (suffix[i * DH : (i + 1) * DH, :] + earlier * recv[head_rows(h), :]).astype(bf16)


def finish_own_kernel(
    k, v, key_near, value_near, suffix, recv, gathered,
    grad_gain, key_done, value_done, key_far, value_far,
    key_own, value_own, total, sems, gain_sem,
):
    half = key_done.shape[0]
    core = core_index()
    near = []
    for base, buffers in ((core, (key_own, value_own)), (1 - core, (key_far, value_far))):
        for i in range(half):
            near.append([
                pltpu.make_async_copy(
                    ref.at[:, col(base * half + i)], buffer.at[i], sems.at[n, len(near)]
                )
                for n, (ref, buffer) in enumerate(zip((key_near, value_near), buffers))
            ])
            for copy in near[-1]:
                copy.start()
    total[...] = jnp.sum(gathered[:, gathered.shape[1] - 8 :], axis=0)
    gain = pltpu.make_async_copy(total, grad_gain, gain_sem)
    gain.start()
    for i in range(half):
        h = core * half + i
        state = finish_state(suffix, recv, i, h)
        for copy in near[i]:
            copy.wait()
        finish_head(h, state, k, v, key_own[i], value_own[i], key_done, value_done, i)
    for copy in sum(near[half:], [gain]):
        copy.wait()


def finish_far_kernel(
    k, v, key_far, value_far, suffix, recv, key_done, value_done,
    grad_key, grad_value, key_buf, value_buf, sems,
):
    half = key_buf.shape[0]
    core = core_index()
    outs = (grad_key, grad_value)
    sent = copy_heads(core * half, half, (key_done, value_done), outs, sems, 0)
    for i in range(half):
        h = (1 - core) * half + i
        state = finish_state(suffix, recv, i, h)
        finish_head(h, state, k, v, key_far[i], value_far[i], key_buf, value_buf, i)
        slots = (key_buf.at[pl.ds(i, 1)], value_buf.at[pl.ds(i, 1)])
        sent += copy_heads(h, 1, slots, outs, sems, half + i)
    for copy in sent:
        copy.wait()


def pack_kernel(states, recv, out, recv_out, buffer, sems):
    peers, rows, _ = out.shape
    count = peers * (rows - 8)
    keep = pltpu.make_async_copy(recv, recv_out, sems.at[0])
    gains = states[2 * count :, :] + recv[2 * count :, :]
    sent = []
    part = peers // 4
    for n in range(4):
        at = slice(n * part, (n + 1) * part)
        size = count // 4
        half = pl.ds(pl.multiple_of(core_index() * count + n * size, size), size)
        near = states[half, :] + recv[half, :]
        buffer[at, : rows - 8, :] = near.reshape(part, rows - 8, DH)
        buffer[at, rows - 8 :, :] = jnp.broadcast_to(gains[None], (part, 8, DH))
        sent.append(pltpu.make_async_copy(buffer.at[at], out.at[at], sems.at[1 + n]))
        sent[-1].start()
        if n == 0:
            keep.start()
    for copy in [keep] + sent:
        copy.wait()


def body(query_rows, key_rows, value_rows, norm_gain, out_grad):
    q, k, v, do = query_rows, key_rows, value_rows, out_grad
    tokens, width = q.shape
    gain = norm_gain.reshape(1, width)
    peers = lax.axis_size("seq")
    chips = peers // 2
    ring = lax.axis_size("head")
    half = width // DH // 2
    state_rows = half * DH
    slice_rows = state_rows // chips
    swap_pairs = [(i, i ^ 1) for i in range(peers)]
    groups = [[2 * i + c for i in range(chips)] for c in range(2)]

    def swap(x):
        return lax.ppermute(x, "seq", swap_pairs)

    def exchange(x):
        return lax.all_to_all(x, "seq", 0, 0, axis_index_groups=groups)

    def scan(x, reverse):
        kernel = functools.partial(scan_kernel, reverse, slice_rows)
        return call(kernel, [((chips, slice_rows, DH), f32)], x)

    slices = ((chips, slice_rows, DH), f32)
    wide = ((tokens, width), f32)
    narrow = ((tokens, width), bf16)
    heads = 2 * half

    def buffers(count, *kinds):
        return [pltpu.VMEM((count, tokens, DH), kind) for kind in kinds]

    states, k_kept, v_kept = call(
        states_kernel, [((width, DH), f32), narrow, narrow], k, v, ins=[HBM, HBM],
        scratch=[pltpu.SemaphoreType.DMA((2, heads))],
    )
    recv = swap(states)
    local = [((tokens, width // 2), f32)]
    (low,) = call(functools.partial(local_kernel, 0), local, q, k_kept, v_kept)
    recv, low, q1 = lax.optimization_barrier((recv, low, q))
    (near,) = call(add_kernel, [slices], states, recv)
    (before,) = scan(exchange(near), False)
    before, q1, k1, v1 = lax.optimization_barrier((exchange(before), q, k_kept, v_kept))
    before = before.reshape(state_rows, DH)
    other = swap(before)
    (high,) = call(functools.partial(local_kernel, half), local, q1, k1, v1)
    att, state_bf, stats = call(
        attend_kernel,
        [wide, ((width, DH), bf16), ((8, tokens), f32)],
        q, low, high, before, other, recv, do, gain,
    )
    parts = [
        lax.ppermute(stats, "head", [(i, (i + d) % ring) for i in range(ring)])
        for d in (1, 3, 2)[: ring - 1]
    ]
    q1, stats = lax.optimization_barrier((q, stats))
    (turned,) = call(turn_kernel, [((width, tokens), bf16)], q1)
    parts.append(stats)
    grad, states = call(
        norm_kernel,
        [narrow, ((width + 8, DH), f32)],
        turned, att, do, gain, *parts, scratch=[pltpu.VMEM((1, width), f32)],
    )
    recv = swap(states)
    attn_out, grad, state_bf = call(
        output_kernel, [narrow, narrow, ((width, DH), bf16)],
        att, gain, *parts, grad, state_bf, places=[HBM] * 3,
        scratch=buffers(heads, bf16) + [pltpu.SemaphoreType.DMA((heads + 2,))],
    )
    recv, attn_out = lax.optimization_barrier((recv, attn_out))
    packed = ((chips, slice_rows + 8, DH), f32)
    packed, recv = call(
        pack_kernel, [packed, ((width + 8, DH), f32)], states, recv, places=[HBM] * 2,
        scratch=[pltpu.VMEM(packed[0], f32), pltpu.SemaphoreType.DMA((5,))],
    )
    packed, recv, q2, k2, v2, grad = lax.optimization_barrier((packed, recv, q, k, v, grad))
    grad_query, key_near, value_near = by_head(
        grads_kernel, [narrow, wide, wide], q2, k2, v2, grad, state_bf
    )
    after, grad_query, key_near, value_near = lax.optimization_barrier(
        (exchange(packed), grad_query, key_near, value_near)
    )
    gathered = after
    (after,) = scan(gathered, True)
    after = exchange(after).reshape(state_rows, DH)
    other = swap(after)
    far = ((half, tokens, DH), f32)
    done = ((half, tokens, DH), bf16)
    grad_gain, key_done, value_done, key_far, value_far = call(
        finish_own_kernel, [((8, DH), f32), done, done, far, far],
        k2, v2, key_near, value_near, after, recv, gathered,
        ins=[VMEM] * 2 + [HBM] * 2 + [VMEM] * 3, places=[HBM] + [VMEM] * 4,
        scratch=buffers(half, f32, f32) + [
            pltpu.VMEM((8, DH), f32),
            pltpu.SemaphoreType.DMA((2, heads)), pltpu.SemaphoreType.DMA,
        ],
    )
    other, key_far, value_far = lax.optimization_barrier((other, key_far, value_far))
    grad_key, grad_value = call(
        finish_far_kernel, [narrow, narrow],
        k2, v2, key_far, value_far, other, recv, key_done, value_done,
        places=[HBM] * 2,
        scratch=buffers(half, bf16, bf16) + [pltpu.SemaphoreType.DMA((2, heads))],
    )
    return attn_out, grad_query, grad_key, grad_value, grad_gain.reshape(width)


def solution(mesh):
    rows, heads = P("seq", "head"), P("head")
    return jax.shard_map(
        body,
        mesh=mesh,
        in_specs=(rows, rows, rows, heads, rows),
        out_specs=(rows, rows, rows, rows, heads),
        check_vma=False,
    )
```

```python
import functools

import jax
import jax.numpy as jnp
from jax import lax
from jax.experimental import pallas as pl
from jax.experimental.pallas import tpu as pltpu
from jax.sharding import PartitionSpec as P

HEADS = 32
DH = 128
COLUMNS = HEADS * DH
EPS = 1e-06

f32 = jnp.float32
bf16 = jnp.bfloat16
VMEM = pl.BlockSpec(memory_space=pltpu.VMEM)
HBM = pl.BlockSpec(memory_space=pltpu.HBM)


def nn(a, b):
    return lax.dot_general(a, b, (((1,), (0,)), ((), ())), preferred_element_type=f32)


def nt(a, b):
    return lax.dot_general(a, b, (((1,), (1,)), ((), ())), preferred_element_type=f32)


def tn(a, b):
    return lax.dot_general(a, b, (((0,), (0,)), ((), ())), preferred_element_type=f32)


def call(kernel, outs, *args, ins=None, places=None, scratch=(), aliases={}):
    ins = ins or [VMEM] * len(args)
    places = places or [VMEM] * len(outs)
    shapes = [
        pltpu.HBM(s, d) if place is HBM else jax.ShapeDtypeStruct(s, d)
        for (s, d), place in zip(outs, places)
    ]
    args = [
        pltpu.with_memory_space_constraint(x, pltpu.HBM) if place is HBM else x
        for x, place in zip(args, ins)
    ]
    return pl.pallas_call(
        kernel,
        out_shape=shapes,
        in_specs=ins,
        out_specs=places,
        scratch_shapes=scratch,
        input_output_aliases=aliases,
        compiler_params=pltpu.CompilerParams(vmem_limit_bytes=24 << 20),
    )(*args)


def core_index():
    return lax.rem(lax.axis_index("seq"), 2)


def col(head):
    return pl.ds(pl.multiple_of(head * DH, DH), DH)


def tri(n, upper):
    row = lax.broadcasted_iota(jnp.int32, (n, n), 0)
    column = lax.broadcasted_iota(jnp.int32, (n, n), 1)
    return column >= row if upper else column <= row


def lower_scores(a, b, mask):
    n = a.shape[0] // 2
    top = jnp.where(mask, nt(a[:n], b[:n]), 0.0).astype(bf16)
    left = nt(a[n:], b[:n]).astype(bf16)
    right = jnp.where(mask, nt(a[n:], b[n:]), 0.0).astype(bf16)
    return top, jnp.concatenate([left, right], axis=1)


def upper_scores(a, b, mask):
    n = a.shape[0] // 2
    left = jnp.where(mask, nt(a[:n], b[:n]), 0.0).astype(bf16)
    right = nt(a[:n], b[n:]).astype(bf16)
    bottom = jnp.where(mask, nt(a[n:], b[n:]), 0.0).astype(bf16)
    return jnp.concatenate([left, right], axis=1), bottom


def head_rows(head):
    return pl.ds(pl.multiple_of(head * DH, DH), DH)


def states_kernel(k, v, q, out, k_kept, v_kept, q_kept, sems, q_sem):
    heads = k.shape[1] // DH
    copies = []
    firsts = list(range(0, heads, 2))
    for h, end in zip(firsts, firsts[1:] + [heads]):
        at = slice(h * DH, end * DH)
        for n, (ref, kept) in enumerate(((k, k_kept), (v, v_kept))):
            copies.append(pltpu.make_async_copy(ref.at[:, at], kept.at[:, at], sems.at[n, h]))
            copies[-1].start()
    queries = pltpu.make_async_copy(q, q_kept, q_sem)
    queries.start()
    for h in range(heads):
        at = slice(h * DH, (h + 1) * DH)
        if h in firsts:
            copies.pop(0).wait()
            copies.pop(0).wait()
        out[at, :] = tn(k_kept[:, at], v_kept[:, at])
    queries.wait()


def add_kernel(states, recv, out):
    rows = out.shape[0] * out.shape[1]
    half = pl.ds(pl.multiple_of(core_index() * rows, rows), rows)
    out[...] = (states[half, :] + recv[half, :]).reshape(out.shape)


def local_kernel(first, q, k, v, out):
    heads = out.shape[1] // DH
    n = q.shape[0] // 2
    mask = tri(n, False)

    def step(h, _):
        top, bottom = lower_scores(q[:, col(first + h)], k[:, col(first + h)], mask)
        vh = v[:, col(first + h)]
        out[:n, col(h)] = nn(top, vh[:n])
        out[n:, col(h)] = nn(bottom, vh)
        return 0

    lax.fori_loop(0, heads, step, 0, unroll=2)


def turn_kernel(q, out):
    def step(h, _):
        out[head_rows(h), :] = q[:, col(h)].T
        return 0

    lax.fori_loop(0, q.shape[1] // DH, step, 0, unroll=2)


def scan_kernel(reverse, rows, x, out):
    peers = x.shape[0]

    run = jnp.zeros(out.shape[1:], f32)
    for at in range(peers - 1, -1, -1) if reverse else range(peers):
        out[at] = run
        run = run + x[at, :rows]


def attend_kernel(q, local_low, local_high, pre, other, recv, do, gain, att, state_bf, stats):
    half = q.shape[1] // DH // 2
    core = core_index()
    later = (core == 1).astype(f32)

    def step(i, sums):
        own, far = pre[head_rows(i), :], other[head_rows(i), :]
        low = jnp.where(core == 0, own, far)
        high = jnp.where(core == 0, far, own)
        squares, dots = sums
        for h, state, local in ((i, low, local_low), (i + half, high, local_high)):
            state = (state + later * recv[head_rows(h), :]).astype(bf16)
            state_bf[head_rows(h), :] = state
            a = local[:, col(i)] + nn(q[:, col(h)], state)
            att[:, col(h)] = a
            squares = squares + a * a
            dots = dots + (do[:, col(h)].astype(f32) * gain[:, col(h)]) * a
        return squares, dots

    zero = jnp.zeros((q.shape[0], DH), f32)
    squares, dots = lax.fori_loop(0, half, step, (zero, zero), unroll=4)
    stats[0:1, :] = jnp.sum(squares.T, axis=0, keepdims=True)
    stats[1:2, :] = jnp.sum(dots.T, axis=0, keepdims=True)


def position_factors(s0, s1, s2, s3):
    sums = s0[...] + s1[...] + s2[...] + s3[...]
    sums = jnp.concatenate([sums, jnp.zeros((6, sums.shape[1]), f32)], axis=0).T
    inverse = lax.rsqrt(sums[:, 0:1] / COLUMNS + EPS)
    mean = sums[:, 1:2] * inverse / COLUMNS
    shape = (sums.shape[0], DH)
    return jnp.broadcast_to(inverse, shape), jnp.broadcast_to(mean, shape)


def norm_kernel(turned, att, do, gain, s0, s1, s2, s3, grad, states, gains):
    heads = att.shape[1] // DH
    inverse, mean = position_factors(s0, s1, s2, s3)

    def step(h, _):
        wide = do[:, col(h)].astype(f32)
        normed = att[:, col(h)] * inverse
        gains[:, col(h)] = jnp.sum(wide * normed, axis=0, keepdims=True)
        g = (inverse * (wide * gain[:, col(h)] - normed * mean)).astype(bf16)
        grad[:, col(h)] = g
        states[head_rows(h), :] = nn(turned[head_rows(h), :], g)
        return 0

    lax.fori_loop(0, heads, step, 0, unroll=8)
    for h in range(heads):
        states[heads * DH + h : heads * DH + h + 1, :] = gains[:, h * DH : (h + 1) * DH]


def output_kernel(att, gain, s0, s1, s2, s3, grad, state_bf, out, grad_out, state_out, rows, sems):
    heads = att.shape[1] // DH
    kept = [
        pltpu.make_async_copy(grad, grad_out, sems.at[heads]),
        pltpu.make_async_copy(state_bf, state_out, sems.at[heads + 1]),
    ]
    for copy in kept:
        copy.start()
    inverse, _ = position_factors(s0, s1, s2, s3)
    for h in range(heads):
        columns = slice(h * DH, (h + 1) * DH)
        rows[h] = (att[:, columns] * inverse * gain[:, columns]).astype(bf16)
        kept.append(pltpu.make_async_copy(rows.at[h], out.at[:, columns], sems.at[h]))
        kept[-1].start()
    for copy in kept:
        copy.wait()


def grads_kernel(q, k, v, grad, state_bf, out, key_near, value_near):
    n = k.shape[0] // 2
    lower, upper = tri(n, False), tri(n, True)
    for h in range(k.shape[1] // DH):
        at = slice(h * DH, (h + 1) * DH)
        g, qh, kh, vh = grad[:, at], q[:, at], k[:, at], v[:, at]
        top, bottom = lower_scores(g, vh, lower)
        far = nt(g, state_bf[at, :])
        out[:n, at] = (far[:n] + nn(top, kh[:n])).astype(bf16)
        out[n:, at] = (far[n:] + nn(bottom, kh)).astype(bf16)
        top, bottom = upper_scores(vh, g, upper)
        key_near[:n, at] = nn(top, qh)
        key_near[n:, at] = nn(bottom, qh[n:])
        top, bottom = upper_scores(kh, qh, upper)
        value_near[:n, at] = nn(top, g)
        value_near[n:, at] = nn(bottom, g[n:])


def by_head(kernel, outs, *args):
    columns = args[0].shape[1]

    def spec(shape):
        if shape[1] == columns:
            return pl.BlockSpec((shape[0], 2 * DH), lambda h: (0, h))
        return pl.BlockSpec((2 * DH, DH), lambda h: (h, 0))

    return pl.pallas_call(
        kernel,
        grid=(columns // DH // 2,),
        out_shape=[pltpu.HBM(s, d) for s, d in outs],
        in_specs=[spec(x.shape) for x in args],
        out_specs=[spec(s) for s, _ in outs],
        compiler_params=pltpu.CompilerParams(vmem_limit_bytes=24 << 20),
    )(*[pltpu.with_memory_space_constraint(x, pltpu.HBM) for x in args])


def finish_head(h, state, k, v, key_near, value_near, key_out, value_out, slot):
    key_out[slot] = (nt(v[:, col(h)], state) + key_near).astype(bf16)
    value_out[slot] = (nn(k[:, col(h)], state) + value_near).astype(bf16)


def copy_heads(base, count, slots, outs, sems, first):
    copies = [
        pltpu.make_async_copy(buffer.at[i], out.at[:, col(base + i)], sems.at[n, first + i])
        for i in range(count)
        for n, (buffer, out) in enumerate(zip(slots, outs))
    ]
    for copy in copies:
        copy.start()
    return copies


def finish_state(suffix, recv, i, h):
    earlier = (core_index() == 0).astype(f32)
    return (suffix[i * DH : (i + 1) * DH, :] + earlier * recv[head_rows(h), :]).astype(bf16)


def finish_own_kernel(
    k, v, key_near, value_near, suffix, recv, gathered,
    grad_gain, key_done, value_done, key_far, value_far,
    key_own, value_own, total, sems, gain_sem,
):
    half = key_done.shape[0]
    core = core_index()
    near = []
    for base, buffers in ((core, (key_own, value_own)), (1 - core, (key_far, value_far))):
        for i in range(half):
            near.append([
                pltpu.make_async_copy(
                    ref.at[:, col(base * half + i)], buffer.at[i], sems.at[n, len(near)]
                )
                for n, (ref, buffer) in enumerate(zip((key_near, value_near), buffers))
            ])
            for copy in near[-1]:
                copy.start()
    total[...] = jnp.sum(gathered[:, gathered.shape[1] - 8 :], axis=0)
    gain = pltpu.make_async_copy(total, grad_gain, gain_sem)
    gain.start()
    for i in range(half):
        h = core * half + i
        state = finish_state(suffix, recv, i, h)
        for copy in near[i]:
            copy.wait()
        finish_head(h, state, k, v, key_own[i], value_own[i], key_done, value_done, i)
    for copy in sum(near[half:], [gain]):
        copy.wait()


def finish_far_kernel(
    k, v, key_far, value_far, suffix, recv, key_done, value_done,
    grad_key, grad_value, key_buf, value_buf, sems,
):
    half = key_buf.shape[0]
    core = core_index()
    outs = (grad_key, grad_value)
    sent = copy_heads(core * half, half, (key_done, value_done), outs, sems, 0)
    for i in range(half):
        h = (1 - core) * half + i
        state = finish_state(suffix, recv, i, h)
        finish_head(h, state, k, v, key_far[i], value_far[i], key_buf, value_buf, i)
        slots = (key_buf.at[pl.ds(i, 1)], value_buf.at[pl.ds(i, 1)])
        sent += copy_heads(h, 1, slots, outs, sems, half + i)
    for copy in sent:
        copy.wait()


def pack_kernel(states, recv, out, recv_out, buffer, sems):
    peers, rows, _ = out.shape
    count = peers * (rows - 8)
    keep = pltpu.make_async_copy(recv, recv_out, sems.at[0])
    gains = states[2 * count :, :] + recv[2 * count :, :]
    sent = []
    part = peers // 4
    for n in range(4):
        at = slice(n * part, (n + 1) * part)
        size = count // 4
        half = pl.ds(pl.multiple_of(core_index() * count + n * size, size), size)
        near = states[half, :] + recv[half, :]
        buffer[at, : rows - 8, :] = near.reshape(part, rows - 8, DH)
        buffer[at, rows - 8 :, :] = jnp.broadcast_to(gains[None], (part, 8, DH))
        sent.append(pltpu.make_async_copy(buffer.at[at], out.at[at], sems.at[1 + n]))
        sent[-1].start()
        if n == 0:
            keep.start()
    for copy in [keep] + sent:
        copy.wait()


def body(query_rows, key_rows, value_rows, norm_gain, out_grad):
    q, k, v, do = query_rows, key_rows, value_rows, out_grad
    tokens, width = q.shape
    gain = norm_gain.reshape(1, width)
    peers = lax.axis_size("seq")
    chips = peers // 2
    ring = lax.axis_size("head")
    half = width // DH // 2
    state_rows = half * DH
    slice_rows = state_rows // chips
    swap_pairs = [(i, i ^ 1) for i in range(peers)]
    groups = [[2 * i + c for i in range(chips)] for c in range(2)]

    def swap(x):
        return lax.ppermute(x, "seq", swap_pairs)

    def exchange(x):
        return lax.all_to_all(x, "seq", 0, 0, axis_index_groups=groups)

    def scan(x, reverse):
        kernel = functools.partial(scan_kernel, reverse, slice_rows)
        return call(kernel, [((chips, slice_rows, DH), f32)], x)

    slices = ((chips, slice_rows, DH), f32)
    wide = ((tokens, width), f32)
    narrow = ((tokens, width), bf16)
    heads = 2 * half

    def buffers(count, *kinds):
        return [pltpu.VMEM((count, tokens, DH), kind) for kind in kinds]

    states, k_kept, v_kept, q_kept = call(
        states_kernel, [((width, DH), f32), narrow, narrow, narrow], k, v, q, ins=[HBM] * 3,
        scratch=[pltpu.SemaphoreType.DMA((2, heads)), pltpu.SemaphoreType.DMA],
    )
    recv = swap(states)
    local = [((tokens, width // 2), f32)]
    (low,) = call(functools.partial(local_kernel, 0), local, q_kept, k_kept, v_kept)
    recv, low = lax.optimization_barrier((recv, low))
    (near,) = call(add_kernel, [slices], states, recv)
    (before,) = scan(exchange(near), False)
    before, q1, k1, v1 = lax.optimization_barrier(
        (exchange(before), q_kept, k_kept, v_kept)
    )
    before = before.reshape(state_rows, DH)
    other = swap(before)
    (high,) = call(functools.partial(local_kernel, half), local, q1, k1, v1)
    att, state_bf, stats = call(
        attend_kernel,
        [wide, ((width, DH), bf16), ((2, tokens), f32)],
        q1, low, high, before, other, recv, do, gain,
    )
    parts = [
        lax.ppermute(stats, "head", [(i, (i + d) % ring) for i in range(ring)])
        for d in (1, 3, 2)[: ring - 1]
    ]
    q1, stats = lax.optimization_barrier((q1, stats))
    (turned,) = call(turn_kernel, [((width, tokens), bf16)], q1)
    parts.append(stats)
    grad, states = call(
        norm_kernel,
        [narrow, ((width + 8, DH), f32)],
        turned, att, do, gain, *parts, scratch=[pltpu.VMEM((1, width), f32)],
    )
    recv = swap(states)
    attn_out, grad, state_bf = call(
        output_kernel, [narrow, narrow, ((width, DH), bf16)],
        att, gain, *parts, grad, state_bf, places=[HBM] * 3,
        scratch=buffers(heads, bf16) + [pltpu.SemaphoreType.DMA((heads + 2,))],
    )
    recv, attn_out = lax.optimization_barrier((recv, attn_out))
    packed = ((chips, slice_rows + 8, DH), f32)
    packed, recv = call(
        pack_kernel, [packed, ((width + 8, DH), f32)], states, recv, places=[HBM] * 2,
        scratch=[pltpu.VMEM(packed[0], f32), pltpu.SemaphoreType.DMA((5,))],
    )
    packed, recv, q2, k2, v2, grad = lax.optimization_barrier((packed, recv, q, k, v, grad))
    grad_query, key_near, value_near = by_head(
        grads_kernel, [narrow, wide, wide], q2, k2, v2, grad, state_bf
    )
    after, grad_query, key_near, value_near = lax.optimization_barrier(
        (exchange(packed), grad_query, key_near, value_near)
    )
    gathered = after
    (after,) = scan(gathered, True)
    after = exchange(after).reshape(state_rows, DH)
    other = swap(after)
    far = ((half, tokens, DH), f32)
    done = ((half, tokens, DH), bf16)
    grad_gain, key_done, value_done, key_far, value_far = call(
        finish_own_kernel, [((8, DH), f32), done, done, far, far],
        k2, v2, key_near, value_near, after, recv, gathered,
        ins=[VMEM] * 2 + [HBM] * 2 + [VMEM] * 3, places=[HBM] + [VMEM] * 4,
        scratch=buffers(half, f32, f32) + [
            pltpu.VMEM((8, DH), f32),
            pltpu.SemaphoreType.DMA((2, heads)), pltpu.SemaphoreType.DMA,
        ],
    )
    other, key_far, value_far = lax.optimization_barrier((other, key_far, value_far))
    grad_key, grad_value = call(
        finish_far_kernel, [narrow, narrow],
        k2, v2, key_far, value_far, other, recv, key_done, value_done,
        places=[HBM] * 2,
        scratch=buffers(half, bf16, bf16) + [pltpu.SemaphoreType.DMA((2, heads))],
    )
    return attn_out, grad_query, grad_key, grad_value, grad_gain.reshape(width)


def solution(mesh):
    rows, heads = P("seq", "head"), P("head")
    return jax.shard_map(
        body,
        mesh=mesh,
        in_specs=(rows, rows, rows, heads, rows),
        out_specs=(rows, rows, rows, rows, heads),
        check_vma=False,
    )
```
